512 devices in a mesh: dp: 64 (over y, x, core), space: 8 (over z).
Axes of the slice: x: 4, y: 8, z: 8, core: 2. Of those that a mesh axis runs over, the one named last changes fastest.
Arguments:
- image: bfloat16 [64, 32, 8, 8, 128], P('dp', 'space'), may hold values from -30 to 30
- cotangent: bfloat16 [64, 32, 8, 8, 128], P('dp', 'space'), may hold values from -30 to 30
- first_weight: bfloat16 [3456, 128], P('dp'), may hold values from -0.109375 to 0.109375
- second_weight: bfloat16 [3456, 128], P('dp'), may hold values from -0.109375 to 0.109375
Outputs:
- output: bfloat16 [64, 32, 8, 8, 128], P('dp', 'space')
- image_grad: bfloat16 [64, 32, 8, 8, 128], P('dp', 'space')
- first_grad: float32 [3456, 128], P('dp')
- second_grad: float32 [3456, 128], P('dp')
The draws below stay inside these ranges and needn't reach their ends.
All inputs are finite; a program needn't handle non-finite values.
Results may differ from the reference program's by a relative error of at most 0.013.
Values may be sent and summed in bfloat16 or wider, within the bound.
No kernel may reach another device: no remote copies, remote signals or barrier semaphores. Data moves between devices by JAX's collectives and lax.ppermute only.
A program may use at most 64 MiB of HBM per device.

```python
import math
import jax
import jax.numpy as jnp
from jax import lax

C = 128
HEIGHT = 8
WIDTH = 8
ROWS = 3456
DEPTH = 32
PATCHES = 64


def depth_ramp(start, finish):
    place = jnp.arange(DEPTH, dtype=jnp.float32) / (DEPTH - 1)
    return (start + (finish - start) * place).reshape(1, DEPTH, 1, 1, 1)


def rough_field(key, start, finish, offset):
    first, second, third = jax.random.split(key, 3)
    shape = (PATCHES, DEPTH, HEIGHT, WIDTH, C)
    base = jax.random.truncated_normal(first, -4.0, 4.0, shape, jnp.float32)
    ramp = depth_ramp(start, finish)
    scales = jnp.exp(jax.random.uniform(second, (C,), jnp.float32, -0.5, 0.5))
    signs = jax.random.uniform(third, (C,), jnp.float32, -1.0, 1.0)
    return ramp * (base * scales + offset * signs)


def draw_image(key, part):
    return rough_field(jax.random.fold_in(key, 11), 1.0, 3.0, 0.5).astype(jnp.bfloat16)


def draw_cotangent(key, part):
    return rough_field(jax.random.fold_in(key, 23), 1.0, 3.0, 0.2).astype(jnp.bfloat16)


def levels(stream_key, extent, cuts, least, high):
    def one(position, shards_of):
        heights = jax.random.uniform(jax.random.fold_in(jax.random.fold_in(stream_key, 6), position), (shards_of,), jnp.float32, least / len(cuts), high / len(cuts))
        return jnp.repeat(jnp.exp(heights), extent[position] // shards_of).reshape((-1,) + (1,) * (len(extent) - position - 1))

    factor_of = one(*cuts[0])
    for cut in cuts[1:]:
        factor_of = factor_of * one(*cut)
    return factor_of


def bell_draw(key, dims, scale, bound, shards=(), kind=jnp.bfloat16):
    loudness = levels(key, dims, shards, -0.22, 0.18) if shards else 1.0
    array = jax.random.normal(key, dims, jnp.float32) * scale * loudness
    return jnp.minimum(jnp.maximum(array, -bound), bound).astype(kind)


def setup_inputs(seed: int = 0) -> dict:
    key_of = jax.random.split(jax.random.key(seed), 5)
    return {
        "image": draw_image(jax.random.fold_in(key_of[4], 71), 0),
        "cotangent": draw_cotangent(jax.random.fold_in(key_of[4], 71), 0),
        "first_weight": bell_draw(key_of[2], (ROWS, C), ROWS ** -0.5, 0.109375, ((0, 64),)),
        "second_weight": bell_draw(key_of[3], (ROWS, C), ROWS ** -0.5, 0.109375, ((0, 64),)),
    }


EPSILON = 1e-05

def gelu_value(values):
    return 0.5 * values * (1.0 + lax.erf(values * 0.7071067811865476))

def gelu_slope(values):
    return 0.5 * (1.0 + lax.erf(values * 0.7071067811865476)) + values * jnp.exp(-0.5 * values * values) * 0.3989422804014327

def product(left, right):
    return jnp.dot(left.astype(jnp.float32), right.astype(jnp.float32), precision=lax.Precision.HIGHEST)

def columns(volume):
    depth, height, width, channels = volume.shape
    padded = jnp.pad(volume, ((1, 1), (1, 1), (1, 1), (0, 0)))
    pieces = [padded[first:first + depth, second:second + height, third:third + width, :] for first in range(3) for second in range(3) for third in range(3)]
    return jnp.concatenate(pieces, axis=-1).reshape(depth * height * width, 27 * channels)

def reverse_taps(weight):
    channels = weight.shape[1]
    return weight.reshape(27, channels, channels)[::-1].transpose(0, 2, 1).reshape(27 * channels, channels)

def normalize(values):
    average = lax.optimization_barrier(jnp.mean(values, axis=0))
    square_mean = lax.optimization_barrier(jnp.mean(values * values, axis=0))
    inverse = lax.rsqrt(square_mean - average * average + EPSILON)
    return ((values - average) * inverse, inverse)

def norm_back(grad, normed, inverse):
    return inverse * (grad - lax.optimization_barrier(jnp.mean(grad, axis=0)) - normed * lax.optimization_barrier(jnp.mean(grad * normed, axis=0)))

def reference(image, cotangent, first_weight, second_weight):
    shape = image.shape[1:]
    cells = shape[0] * shape[1] * shape[2]

    def one_patch(carry, item):
        volume, outer = item
        first_columns = columns(volume)
        first_norm, first_inverse = normalize(product(first_columns, first_weight))
        hidden = gelu_value(first_norm).astype(jnp.bfloat16)
        second_columns = columns(hidden.reshape(shape))
        second_norm, second_inverse = normalize(product(second_columns, second_weight))
        summed = volume.reshape(cells, C).astype(jnp.float32) + second_norm
        output = gelu_value(summed).astype(jnp.bfloat16)
        outer_grad = outer.reshape(cells, C).astype(jnp.float32) * gelu_slope(summed)
        second_delta = norm_back(outer_grad, second_norm, second_inverse).astype(jnp.bfloat16)
        second_part = product(second_columns.T, second_delta)
        inner_grad = product(columns(second_delta.reshape(shape)), reverse_taps(second_weight))
        first_delta = norm_back(inner_grad * gelu_slope(first_norm), first_norm, first_inverse).astype(jnp.bfloat16)
        first_part = product(first_columns.T, first_delta)
        image_grad = (outer_grad + product(columns(first_delta.reshape(shape)), reverse_taps(first_weight))).astype(jnp.bfloat16)
        return ((carry[0] + first_part, carry[1] + second_part), (output.reshape(shape), image_grad.reshape(shape)))
    zeros = jnp.zeros((ROWS, C), jnp.float32)
    totals, results = lax.scan(one_patch, (zeros, zeros), (image, cotangent))
    factor = 1.0 / math.sqrt(PATCHES * DEPTH * HEIGHT * WIDTH)
    return (results[0], results[1], totals[0] * factor, totals[1] * factor)
```

```python
import functools
import math

import jax
import jax.numpy as jnp
from jax import lax
from jax.experimental import pallas as pl
from jax.experimental.pallas import tpu as pltpu
from jax.sharding import Mesh, PartitionSpec as P


EPSILON = 1e-05
C = 128
H = 8
W = 8
PLANE = H * W
TAPS = 27
NINE = 9 * C
ROWS = TAPS * C
BLOCK = 256
MATRIX = 512
SPLIT = 8

bf16 = jnp.bfloat16
f32 = jnp.float32


def phi_parts(u):
    cdf = 0.5 * (1.0 + lax.erf(u * 0.7071067811865476))
    return cdf


def slope_of(u, cdf):
    return cdf + u * jnp.exp(-0.5 * u * u) * 0.3989422804014327


def shifts_of(x):
    w_at = lax.broadcasted_iota(jnp.int32, x.shape, 2)
    left = jnp.where(w_at >= 1, pltpu.roll(x, 1, axis=2), 0.0)
    right = jnp.where(w_at <= W - 2, pltpu.roll(x, W - 1, axis=2), 0.0)
    zero = jnp.zeros_like(x[:, :1])
    out = []
    for b in range(3):
        for y in (left, x, right):
            if b == 0:
                y = jnp.concatenate([zero, y[:, : H - 1]], axis=1)
            elif b == 2:
                y = jnp.concatenate([y[:, 1:], zero], axis=1)
            out.append(y)
    return out


def build_nine(load, nine, planes, first=0):
    step = 2

    def one(i, _):
        x = load(i * step, step).astype(f32).reshape(step, H, W, C)
        row = pl.multiple_of((i * step + 1 + first) * PLANE, PLANE)
        for k, y in enumerate(shifts_of(x)):
            nine[pl.ds(row, step * PLANE), k * C : (k + 1) * C] = y.reshape(
                step * PLANE, C
            ).astype(bf16)
        return 0

    lax.fori_loop(0, planes // step, one, 0)


def clear_ends(nine, planes):
    zero = jnp.zeros((PLANE, NINE), bf16)
    nine[0:PLANE, :] = zero
    nine[(planes + 1) * PLANE : (planes + 2) * PLANE, :] = zero


def plane_loader(ref):
    return lambda d, n: ref[pl.ds(pl.multiple_of(d * PLANE, PLANE), n * PLANE), :]


def conv_rows(nine, weight, row, rows):
    acc = None
    for a in range(3):
        part = jnp.dot(
            nine[pl.ds(pl.multiple_of(row + a * PLANE, PLANE), rows), :],
            weight[a * NINE : (a + 1) * NINE, :],
            preferred_element_type=f32,
        )
        acc = part if acc is None else acc + part
    return acc


def reverse_into(weight, out):
    for k in range(TAPS):
        block = weight[(TAPS - 1 - k) * C : (TAPS - k) * C, :]
        out[k * C : (k + 1) * C, :] = block.astype(f32).T.astype(bf16)


def assemble(core, mine, theirs, flat, weight):
    chips = mine.shape[0]
    part = ROWS // (2 * chips)
    mine_first = core == 0
    for y in range(chips):
        one = mine[y].astype(f32)
        two = theirs[y].astype(f32)
        even = jnp.where(mine_first, one, two)[:part]
        odd = jnp.where(mine_first, two, one)[:part]
        flat[2 * y * part : (2 * y + 1) * part, :] = even
        flat[(2 * y + 1) * part : (2 * y + 2) * part, :] = odd
    for k in range(TAPS):
        weight[k * C : (k + 1) * C, :] = flat[k * C : (k + 1) * C, :].astype(bf16)


def row_sum(x):
    return jnp.sum(x, axis=0, keepdims=True)


def grad_into(nine, delta, cells, three, turned, flat, out, place):
    rows = cells + 2 * PLANE
    for a in range(3):
        cols = slice(a * C, (a + 1) * C)
        if a:
            three[0 : a * PLANE, cols] = jnp.zeros((a * PLANE, C), bf16)
        three[a * PLANE : a * PLANE + cells, cols] = delta[...]
        if a < 2:
            three[a * PLANE + cells : rows, cols] = jnp.zeros(((2 - a) * PLANE, C), bf16)

    def turn(i, _):
        at = pl.multiple_of(i * C, C)
        for a in range(3):
            block = three[pl.ds(at, C), a * C : (a + 1) * C].astype(f32)
            turned[a * C : (a + 1) * C, pl.ds(at, C)] = block.T.astype(bf16)
        return 0

    lax.fori_loop(0, rows // C, turn, 0)

    def product(n, _):
        at = pl.multiple_of(n * 3 * C, 3 * C)
        total = jnp.dot(
            turned[...], nine[:, pl.ds(at, 3 * C)], preferred_element_type=f32
        )
        for a in range(3):
            for i in range(3):
                block = total[a * C : (a + 1) * C, i * C : (i + 1) * C].T
                flat[pl.ds(pl.multiple_of(a * NINE + at + i * C, C), C), :] = block
        return 0

    lax.fori_loop(0, 3, product, 0)
    shares, tall, _ = out.shape
    part = ROWS // shares
    base = place[0] * (-(-part // SPLIT))
    for j in range(shares):
        out[j] = flat[pl.ds(j * part + base, tall), :].astype(bf16)


def first_kernel(
    place, image, mine, theirs,
    normed, hidden, inverse_out, weight,
    nine, conv, flat,
):
    cells = image.shape[0]
    planes = cells // PLANE
    assemble(place[1], mine, theirs, flat, weight)
    clear_ends(nine, planes)
    build_nine(plane_loader(image), nine, planes)

    def one(i, sums):
        row = pl.multiple_of(i * MATRIX, MATRIX)
        acc = conv_rows(nine, weight, row, MATRIX)
        conv[pl.ds(row, MATRIX), :] = acc
        return (sums[0] + row_sum(acc), sums[1] + row_sum(acc * acc))

    zero = jnp.zeros((1, C), f32)
    total, square = lax.fori_loop(0, cells // MATRIX, one, (zero, zero))
    average = total / cells
    inverse = lax.rsqrt(square / cells - average * average + EPSILON)
    inverse_out[...] = jnp.broadcast_to(inverse, inverse_out.shape)

    def two(i, _):
        at = pl.ds(pl.multiple_of(i * BLOCK, BLOCK), BLOCK)
        u = (conv[at, :] - average) * inverse
        normed[at, :] = u
        hidden[at, :] = (u * phi_parts(u)).astype(bf16)
        return 0

    lax.fori_loop(0, cells // BLOCK, two, 0)


def second_kernel(
    place, hidden, mine, theirs, image, cotangent,
    output, outer_slab, delta, grads, weight,
    nine, conv, outer, three, turned, flat,
):
    cells = hidden.shape[0]
    planes = cells // PLANE
    assemble(place[1], mine, theirs, flat, weight)
    clear_ends(nine, planes)
    build_nine(plane_loader(hidden), nine, planes)

    def one(i, sums):
        row = pl.multiple_of(i * MATRIX, MATRIX)
        acc = conv_rows(nine, weight, row, MATRIX)
        conv[pl.ds(row, MATRIX), :] = acc
        return (sums[0] + row_sum(acc), sums[1] + row_sum(acc * acc))

    zero = jnp.zeros((1, C), f32)
    total, square = lax.fori_loop(0, cells // MATRIX, one, (zero, zero))
    average = total / cells
    inverse = lax.rsqrt(square / cells - average * average + EPSILON)
    slab = output.shape[0]

    def two(i, sums):
        at = pl.ds(pl.multiple_of(i * slab, slab), slab)
        n = (conv[at, :] - average) * inverse
        conv[at, :] = n
        u = image[at, :].astype(f32) + n
        cdf = phi_parts(u)
        grad = cotangent[at, :].astype(f32) * slope_of(u, cdf)
        outer[at, :] = grad

        @pl.when(i == place[0])
        def _():
            output[...] = (u * cdf).astype(bf16)
            outer_slab[...] = grad

        return (sums[0] + row_sum(grad), sums[1] + row_sum(grad * n))

    plain, paired = lax.fori_loop(0, cells // slab, two, (zero, zero))
    plain = plain / cells
    paired = paired / cells

    def three_(i, _):
        at = pl.ds(pl.multiple_of(i * BLOCK, BLOCK), BLOCK)
        delta[at, :] = (inverse * (outer[at, :] - plain - conv[at, :] * paired)).astype(bf16)
        return 0

    lax.fori_loop(0, cells // BLOCK, three_, 0)
    grad_into(nine, delta, cells, three, turned, flat, grads, place)


def third_kernel(
    place, second_delta, weight, normed, inverse, image,
    delta, grads,
    nine, conv, turned_weight, three, turned, flat,
):
    cells = image.shape[0]
    planes = cells // PLANE
    clear_ends(nine, planes)
    reverse_into(weight, turned_weight)
    build_nine(plane_loader(second_delta), nine, planes)

    def one(i, sums):
        row = pl.multiple_of(i * MATRIX, MATRIX)
        at = pl.ds(row, MATRIX)
        acc = conv_rows(nine, turned_weight, row, MATRIX)
        u = normed[at, :]
        grad = acc * slope_of(u, phi_parts(u))
        conv[at, :] = grad
        return (sums[0] + row_sum(grad), sums[1] + row_sum(grad * u))

    zero = jnp.zeros((1, C), f32)
    plain, paired = lax.fori_loop(0, cells // MATRIX, one, (zero, zero))
    plain = plain / cells
    paired = paired / cells
    scale = inverse[0:1, :]

    def two(i, _):
        at = pl.ds(pl.multiple_of(i * BLOCK, BLOCK), BLOCK)
        delta[at, :] = (scale * (conv[at, :] - plain - normed[at, :] * paired)).astype(bf16)
        return 0

    lax.fori_loop(0, cells // BLOCK, two, 0)
    build_nine(plane_loader(image), nine, planes)
    grad_into(nine, delta, cells, three, turned, flat, grads, place)


def fourth_kernel(place, delta, weight, outer_slab, grad, nine, turned_weight):
    slab = grad.shape[0]
    planes = slab // PLANE
    last = delta.shape[0] // PLANE
    reverse_into(weight, turned_weight)
    base = place[0] * planes
    for p in range(planes + 2):
        d = base + (p - 1)
        inside = jnp.logical_and(d >= 0, d < last)
        at = pl.multiple_of(jnp.clip(d, 0, last - 1) * PLANE, PLANE)
        x = delta[pl.ds(at, PLANE), :].astype(f32)
        x = jnp.where(inside, x, 0.0).reshape(1, H, W, C)
        for k, y in enumerate(shifts_of(x)):
            nine[p * PLANE : (p + 1) * PLANE, k * C : (k + 1) * C] = y.reshape(
                PLANE, C
            ).astype(bf16)
    grad[...] = (outer_slab[...] + conv_rows(nine, turned_weight, 0, slab)).astype(bf16)


SMEM = pl.BlockSpec(memory_space=pltpu.SMEM)
VMEM = pl.BlockSpec(memory_space=pltpu.VMEM)


def call(kernel, outs, scratch, *args, mib=4):
    specs = []
    for a in args:
        if isinstance(a, tuple):
            whole, half = a
            shape = (whole.shape[0], whole.shape[1] // 2, C)
            specs.append(pl.BlockSpec(shape, functools.partial(lambda h, i: (0, h, 0), half)))
        else:
            specs.append(SMEM if a.dtype == jnp.int32 else VMEM)
    args = [a[0] if isinstance(a, tuple) else a for a in args]
    return pl.pallas_call(
        kernel,
        grid=(1,),
        out_shape=tuple(jax.ShapeDtypeStruct(s, d) for s, d in outs),
        in_specs=specs,
        out_specs=tuple(VMEM for _ in outs),
        scratch_shapes=[pltpu.VMEM(s, d) for s, d in scratch],
        compiler_params=pltpu.CompilerParams(vmem_limit_bytes=mib * 1024 * 1024),
    )(*args)


def first_call(place, image, mine, theirs):
    cells = image.shape[0]
    return call(
        first_kernel,
        [((cells, C), f32), ((cells, C), bf16), ((8, C), f32), ((ROWS, C), bf16)],
        [((cells + 2 * PLANE, NINE), bf16), ((cells, C), f32), ((ROWS + 8, C), f32)],
        place, image, (mine, 0), (theirs, 0), mib=16,
    )


def grad_scratch(cells):
    return [
        ((cells + 2 * PLANE, 3 * C), bf16),
        ((3 * C, cells + 2 * PLANE), bf16),
        ((ROWS + 8, C), f32),
    ]


def second_call(place, hidden, mine, theirs, image, cotangent, slab, chunks):
    cells = hidden.shape[0]
    return call(
        second_kernel,
        [
            ((slab, C), bf16), ((slab, C), f32), ((cells, C), bf16), (chunks, bf16),
            ((ROWS, C), bf16),
        ],
        [((cells + 2 * PLANE, NINE), bf16), ((cells, C), f32), ((cells, C), f32)]
        + grad_scratch(cells),
        place, hidden, (mine, 1), (theirs, 1), image, cotangent, mib=24,
    )


def third_call(place, second_delta, weight, normed, inverse, image, chunks):
    cells = image.shape[0]
    return call(
        third_kernel,
        [((cells, C), bf16), (chunks, bf16)],
        [((cells + 2 * PLANE, NINE), bf16), ((cells, C), f32), ((ROWS, C), bf16)]
        + grad_scratch(cells),
        place, second_delta, weight, normed, inverse, image, mib=24,
    )


def fourth_call(place, delta, weight, outer_slab):
    slab = outer_slab.shape[0]
    return call(
        fourth_kernel,
        [((slab, C), bf16)],
        [((slab + 2 * PLANE, NINE), bf16), ((ROWS, C), bf16)],
        place, delta, weight, outer_slab, mib=8,
    )[0]


def total_kernel(factor, first, second, both):
    tall = first.shape[1]
    for n, x in enumerate((first, second)):
        both[n * tall : (n + 1) * tall, :] = jnp.sum(x[...].astype(f32), axis=0) * factor


def total_call(first, second, factor):
    tall = first.shape[1]
    return call(
        functools.partial(total_kernel, factor),
        [((2 * tall, C), f32)], [], first, second,
    )[0]


def join_kernel(pieces, first, second):
    split, both, _ = pieces.shape
    tall = both // 2
    part = first.shape[0]
    piece = -(-part // split)
    for n, out in enumerate((first, second)):
        for s in range(split):
            rows = min(piece, part - s * piece)
            out[s * piece : s * piece + rows, :] = pieces[s, n * tall : n * tall + rows, :]


def join_call(pieces, part):
    return call(join_kernel, [((part, C), f32), ((part, C), f32)], [], pieces)


def spread(x, axes, count):
    copies = jnp.broadcast_to(x[None], (count,) + x.shape)
    return lax.all_to_all(copies, axes, 0, 0, tiled=True)


def solution(mesh):
    dp, space = mesh.shape["dp"], mesh.shape["space"]
    across = 4
    fine = Mesh(
        mesh.devices.reshape(dp // (2 * across), across, 2, space),
        ("y", "x", "core", "space"),
    )
    chips = dp // 2
    swap = [(0, 1), (1, 0)]
    plane = ("y", "x", "core")

    def step(image, cotangent, first_weight, second_weight):
        slab = image.shape[1] * PLANE
        cells = slab * space
        part = first_weight.shape[0]
        padded = -(-part // 8) * 8
        piece = -(-part // space)
        chunks = (dp, -(-piece // 8) * 8, C)
        factor = 1.0 / math.sqrt(cells * dp)
        core = lax.axis_index("core")
        place = jnp.stack([lax.axis_index("space"), core]).astype(jnp.int32)

        tall = ((0, padded - part), (0, 0))
        shard = jnp.concatenate([jnp.pad(first_weight, tall), jnp.pad(second_weight, tall)])
        mine = spread(shard, ("y", "x"), chips)
        patch = lax.all_gather(image.reshape(slab, C), "space", axis=0, tiled=True)
        theirs = lax.ppermute(mine, "core", swap)
        outer = spread(cotangent.reshape(slab, C), "space", space).reshape(cells, C)
        normed, hidden, inverse, w1 = first_call(place, patch, mine, theirs)
        output, outer_slab, second_delta, grads2, w2 = second_call(
            place, hidden, mine, theirs, patch, outer, slab, chunks
        )
        parts2 = lax.all_to_all(grads2, plane, 0, 0, tiled=True)
        first_delta, grads1 = third_call(
            place, second_delta, w2, normed, inverse, patch, chunks
        )
        parts1 = lax.all_to_all(grads1, plane, 0, 0, tiled=True)
        image_grad = fourth_call(place, first_delta, w1, outer_slab)
        pieces = spread(total_call(parts1, parts2, factor), "space", space)
        first_grad, second_grad = join_call(pieces, part)
        return (
            output.reshape(image.shape),
            image_grad.reshape(image.shape),
            first_grad,
            second_grad,
        )

    dp_axes = ("y", "x", "core")
    field = P(dp_axes, "space", None, None, None)
    rows = P(dp_axes, None)
    return jax.shard_map(
        step,
        mesh=fine,
        in_specs=(field, field, rows, rows),
        out_specs=(field, field, rows, rows),
        check_vma=False,
    )
```

```python
import functools
import math

import jax
import jax.numpy as jnp
from jax import lax
from jax.experimental import pallas as pl
from jax.experimental.pallas import tpu as pltpu
from jax.sharding import Mesh, PartitionSpec as P


EPSILON = 1e-05
C = 128
H = 8
W = 8
PLANE = H * W
TAPS = 27
NINE = 9 * C
ROWS = TAPS * C
BLOCK = 128
STEP = 16
SPLIT = 8

bf16 = jnp.bfloat16
f32 = jnp.float32


def phi_parts(u):
    cdf = 0.5 * (1.0 + lax.erf(u * 0.7071067811865476))
    return cdf


def slope_of(u, cdf):
    return cdf + u * jnp.exp(-0.5 * u * u) * 0.3989422804014327


def put_w_shifts(value, out, row):
    rows = value.shape[0]
    x = value.reshape(rows // PLANE, H, W, C)
    w_at = lax.broadcasted_iota(jnp.int32, x.shape, 2)
    left = jnp.where(w_at >= 1, pltpu.roll(x, 1, axis=2), 0.0)
    right = jnp.where(w_at <= W - 2, pltpu.roll(x, W - 1, axis=2), 0.0)
    for c, y in enumerate((left, x, right)):
        out[pl.ds(row, rows), c * C : (c + 1) * C] = y.reshape(rows, C).astype(bf16)


def h_down(x):
    return jnp.concatenate([jnp.zeros_like(x[:, :1]), x[:, : H - 1]], axis=1)


def h_up(x):
    return jnp.concatenate([x[:, 1:], jnp.zeros_like(x[:, :1])], axis=1)


def put_h_shifts(value, out, row):
    rows = value.shape[0]
    x = value.reshape(rows // PLANE, H, W, C)
    for b, y in enumerate((h_up(x), x, h_down(x))):
        out[pl.ds(row, rows), b * C : (b + 1) * C] = y.reshape(rows, C).astype(bf16)


def conv_into(acc, source, weight, planes, step):
    rows = step * PLANE

    margin = 2 * PLANE

    def clear(i, _):
        at = pl.ds(pl.multiple_of(i * margin, margin), margin)
        acc[at, :] = jnp.zeros((margin, C), f32)
        return 0

    lax.fori_loop(0, (planes + 2) // 2, clear, 0)

    def one(i, _):
        row = pl.multiple_of(i * rows, rows)
        z = jnp.dot(source[pl.ds(row, rows), :], weight[...], preferred_element_type=f32)
        for a in range(3):
            x = [
                z[:, (3 * a + b) * C : (3 * a + b + 1) * C].reshape(step, H, W, C)
                for b in range(3)
            ]
            total = h_down(x[0]) + x[1] + h_up(x[2])
            at = pl.ds(pl.multiple_of(row + (2 - a) * PLANE, PLANE), rows)
            acc[at, :] += total.reshape(rows, C)
        return 0

    lax.fori_loop(0, planes // step, one, 0)


def by_taps(flat, weight):
    for k in range(TAPS):
        c, ab = k % 3, k // 3
        weight[c * C : (c + 1) * C, ab * C : (ab + 1) * C] = flat[
            k * C : (k + 1) * C, :
        ].astype(bf16)


def reverse_into(weight, out):
    for k in range(TAPS):
        c, ab = k % 3, k // 3
        block = weight[(2 - c) * C : (3 - c) * C, (8 - ab) * C : (9 - ab) * C]
        out[c * C : (c + 1) * C, ab * C : (ab + 1) * C] = block.T


def assemble(core, mine, theirs, flat, weight):
    chips = mine.shape[0]
    part = ROWS // (2 * chips)
    mine_first = core == 0
    for y in range(chips):
        one = mine[y].astype(f32)
        two = theirs[y].astype(f32)
        even = jnp.where(mine_first, one, two)[:part]
        odd = jnp.where(mine_first, two, one)[:part]
        flat[2 * y * part : (2 * y + 1) * part, :] = even
        flat[(2 * y + 1) * part : (2 * y + 2) * part, :] = odd
    by_taps(flat, weight)


def row_sum(x):
    return jnp.sum(x, axis=0, keepdims=True)


def turn_into(source, turned):
    many = 4

    def turn(i, _):
        for n in range(many):
            at = pl.multiple_of((i * many + n) * C, C)
            for c in range(3):
                block = source[pl.ds(at, C), c * C : (c + 1) * C]
                turned[c * C : (c + 1) * C, pl.ds(at, C)] = block.T
        return 0

    lax.fori_loop(0, source.shape[0] // (many * C), turn, 0)


def grad_into(turned, delta, cells, flat, out, place, top):
    def shifted(a, first, last):
        row = (2 - a) * PLANE
        return delta[row : row + cells, first * C : last * C]

    jobs = [([(a, 0), (a, 1)], lambda a=a: shifted(a, 0, 2)) for a in range(3)]
    jobs.append(
        ([(0, 2), (1, 2)], lambda: jnp.concatenate([shifted(0, 2, 3), shifted(1, 2, 3)], axis=1))
    )
    jobs.append(([(2, 2)], lambda: shifted(2, 2, 3)))
    for taps, side in jobs:
        total = jnp.dot(turned[...], side(), preferred_element_type=f32)
        for n, (a, b) in enumerate(taps):
            for c in range(3):
                row = (9 * a + 3 * b + c) * C
                flat[row : row + C, :] = total[c * C : (c + 1) * C, n * C : (n + 1) * C]
    near, far, tall, _ = out.shape
    part = ROWS // (near * far)
    tall = tall // 2
    base = place[0] * (-(-part // SPLIT))
    for j in range(near * far):
        chunk = flat[pl.ds(j * part + base, tall), :].astype(bf16)
        out[j % near, j // near, top : top + tall, :] = chunk


def blocks_of(cells, body, init, rows=BLOCK):
    def one(i, carry):
        return body(i, pl.multiple_of(i * rows, rows), carry)

    return lax.fori_loop(0, cells // rows, one, init)


def statistics(conv, cells):
    zero = jnp.zeros((1, C), f32)

    def one(i, row, sums):
        acc = conv[pl.ds(row + PLANE, 4 * BLOCK), :]
        return (sums[0] + row_sum(acc), sums[1] + row_sum(acc * acc))

    total, square = blocks_of(cells, one, (zero, zero), 4 * BLOCK)
    average = total / cells
    return average, lax.rsqrt(square / cells - average * average + EPSILON)


def main_kernel(offsets, place, *refs):
    blocks, refs = refs[: len(offsets)], refs[len(offsets) :]
    (
        mine, theirs,
        output, outer_out, delta_out, grads_out, weight_out,
        image, cotangent, first_delta, outer_slab, grads,
        mine1, theirs1, mine2, theirs2, weight1, weight2, turned_weight,
        image_three, three, delta_three, turned, normed, conv, outer, flat,
        image_sem, other_sem, weight_sem, out_sem,
    ) = refs
    cells = image.shape[0]
    planes = cells // PLANE
    slab = output.shape[0]
    count = cells // slab
    padded = mine1.shape[1]
    zero = jnp.zeros((1, C), f32)
    copy = pltpu.make_async_copy
    fields = ([], [])
    for n, ((offset, index), block) in enumerate(zip(offsets, blocks)):
        owner = lax.rem(place[0] + (offset + count), count)
        at = pl.ds(pl.multiple_of(owner * slab, slab), slab)
        row = 2 * index * slab
        fields[0].append(copy(block.at[row : row + slab], image.at[at], image_sem.at[n]))
        fields[1].append(
            copy(block.at[row + slab : row + 2 * slab], cotangent.at[at], other_sem.at[n])
        )
    weights = [
        copy(source.at[:, half * padded : (half + 1) * padded], target, weight_sem.at[n])
        for n, (source, half, target) in enumerate(
            ((mine, 0, mine1), (theirs, 0, theirs1), (mine, 1, mine2), (theirs, 1, theirs2))
        )
    ]
    for c in fields[0] + weights + fields[1]:
        c.start()
    edge = jnp.zeros((PLANE, 3 * C), bf16)
    delta_three[0:PLANE, :] = edge
    delta_three[cells + PLANE : cells + 2 * PLANE, :] = edge
    for c in fields[0]:
        c.wait()

    def shift_image(i, row, _):
        put_w_shifts(image[pl.ds(row, BLOCK), :].astype(f32), image_three, row)
        return 0

    blocks_of(cells, shift_image, 0)
    for c in weights[:2]:
        c.wait()
    assemble(place[1], mine1, theirs1, flat, weight1)
    weight_copy = copy(weight1, weight_out, out_sem.at[0])
    weight_copy.start()
    conv_into(conv, image_three, weight1, planes, STEP)
    average1, inverse1 = statistics(conv, cells)

    def norm_one(i, row, _):
        u = (conv[pl.ds(row + PLANE, BLOCK), :] - average1) * inverse1
        normed[pl.ds(row, BLOCK), :] = u
        put_w_shifts(u * phi_parts(u), three, row)
        return 0

    blocks_of(cells, norm_one, 0)
    for c in weights[2:]:
        c.wait()
    assemble(place[1], mine2, theirs2, flat, weight2)
    conv_into(conv, three, weight2, planes, STEP)
    average, inverse = statistics(conv, cells)
    turn_into(three, turned)
    for c in fields[1]:
        c.wait()
    parts = slab // BLOCK

    def norm_two(i, row, sums):
        at = pl.ds(row, BLOCK)
        n = (conv[pl.ds(row + PLANE, BLOCK), :] - average) * inverse
        conv[pl.ds(row + PLANE, BLOCK), :] = n
        u = image[at, :].astype(f32) + n
        cdf = phi_parts(u)
        grad = cotangent[at, :].astype(f32) * slope_of(u, cdf)
        outer[at, :] = grad

        @pl.when(lax.div(i, parts) == place[0])
        def _():
            inner = pl.ds(pl.multiple_of(lax.rem(i, parts) * BLOCK, BLOCK), BLOCK)
            output[inner, :] = (u * cdf).astype(bf16)
            outer_slab[inner, :] = grad

        return (sums[0] + row_sum(grad), sums[1] + row_sum(grad * n))

    plain, paired = blocks_of(cells, norm_two, (zero, zero))
    outer_copy = copy(outer_slab, outer_out, out_sem.at[1])
    outer_copy.start()
    plain = plain / cells
    paired = paired / cells

    def back_two(i, row, _):
        n = conv[pl.ds(row + PLANE, BLOCK), :]
        value = inverse * (outer[pl.ds(row, BLOCK), :] - plain - n * paired)
        put_w_shifts(value, three, row)
        put_h_shifts(value, delta_three, row + PLANE)
        return 0

    blocks_of(cells, back_two, 0)
    half = grads.shape[2] // 2
    grad_into(turned, delta_three, cells, flat, grads, place, half)

    reverse_into(weight2, turned_weight)
    conv_into(conv, three, turned_weight, planes, STEP)

    def inner_grad(i, row, sums):
        u = normed[pl.ds(row, BLOCK), :]
        grad = conv[pl.ds(row + PLANE, BLOCK), :] * slope_of(u, phi_parts(u))
        conv[pl.ds(row + PLANE, BLOCK), :] = grad
        return (sums[0] + row_sum(grad), sums[1] + row_sum(grad * u))

    plain1, paired1 = blocks_of(cells, inner_grad, (zero, zero))
    plain1 = plain1 / cells
    paired1 = paired1 / cells

    def back_one(i, row, _):
        at = pl.ds(row, BLOCK)
        grad = conv[pl.ds(row + PLANE, BLOCK), :]
        value = inverse1 * (grad - plain1 - normed[at, :] * paired1)
        first_delta[at, :] = value.astype(bf16)
        put_h_shifts(value, delta_three, row + PLANE)
        return 0

    blocks_of(cells, back_one, 0)
    delta_copy = copy(first_delta, delta_out, out_sem.at[2])
    delta_copy.start()
    turn_into(image_three, turned)
    grad_into(turned, delta_three, cells, flat, grads, place, 0)
    grads_copy = copy(grads, grads_out, out_sem.at[3])
    grads_copy.start()
    for c in (weight_copy, outer_copy, delta_copy, grads_copy):
        c.wait()


def fourth_kernel(place, delta, weight, outer_slab, grad, three, conv, turned_weight):
    slab = grad.shape[0]
    planes = slab // PLANE
    last = delta.shape[0] // PLANE
    reverse_into(weight, turned_weight)
    base = place[0] * planes
    for p in range(planes + 2):
        d = base + (p - 1)
        inside = jnp.logical_and(d >= 0, d < last)
        at = pl.multiple_of(jnp.clip(d, 0, last - 1) * PLANE, PLANE)
        x = delta[pl.ds(at, PLANE), :].astype(f32)
        put_w_shifts(jnp.where(inside, x, 0.0), three, p * PLANE)
    conv_into(conv, three, turned_weight, planes + 2, planes + 2)
    total = conv[2 * PLANE : 2 * PLANE + slab, :]
    grad[...] = (outer_slab[...] + total).astype(bf16)


SMEM = pl.BlockSpec(memory_space=pltpu.SMEM)
VMEM = pl.BlockSpec(memory_space=pltpu.VMEM)
HBM = pl.BlockSpec(memory_space=pltpu.HBM)


def call(kernel, outs, scratch, *args, mib=4, far_in=(), far_out=()):
    specs = [
        HBM if n in far_in else SMEM if a.dtype == jnp.int32 else VMEM
        for n, a in enumerate(args)
    ]
    args = [
        pltpu.with_memory_space_constraint(a, pltpu.HBM) if n in far_in else a
        for n, a in enumerate(args)
    ]
    return pl.pallas_call(
        kernel,
        out_shape=tuple(jax.ShapeDtypeStruct(s, d) for s, d in outs),
        in_specs=specs,
        out_specs=tuple(HBM if n in far_out else VMEM for n in range(len(outs))),
        scratch_shapes=scratch,
        compiler_params=pltpu.CompilerParams(vmem_limit_bytes=mib * 1024 * 1024),
    )(*args)


def main_call(place, blocks, mine, theirs, slab, chunks):
    count = sum(len(offsets) for offsets, _ in blocks)
    cells = slab * count
    offsets = [(o, n) for many, _ in blocks for n, o in enumerate(many)]
    arrays = [array for many, array in blocks for _ in many]
    field = (cells, C)
    half = (mine.shape[0], mine.shape[1] // 2, C)
    local = pltpu.VMEM
    signal = pltpu.SemaphoreType.DMA
    return call(
        functools.partial(main_kernel, offsets),
        [
            ((slab, C), bf16), ((slab, C), f32), (field, bf16), (chunks, bf16),
            ((3 * C, NINE), bf16),
        ],
        [local(field, bf16)] * 3
        + [local((slab, C), f32), local(chunks, bf16)]
        + [local(half, bf16)] * 4
        + [local((3 * C, NINE), bf16)] * 3
        + [
            local((cells, 3 * C), bf16), local((cells, 3 * C), bf16),
            local((cells + 2 * PLANE, 3 * C), bf16), local((3 * C, cells), bf16),
            local(field, f32), local((cells + 2 * PLANE, C), f32), local(field, f32),
            local((ROWS + 8, C), f32),
            signal((count,)), signal((count,)), signal((4,)), signal((4,)),
        ],
        place, *arrays, mine, theirs,
        mib=32, far_in=range(1, count + 3), far_out=(1, 2, 3, 4),
    )


def fourth_call(place, delta, weight, outer_slab):
    slab = outer_slab.shape[0]
    return call(
        fourth_kernel,
        [((slab, C), bf16)],
        [
            pltpu.VMEM((slab + 2 * PLANE, 3 * C), bf16),
            pltpu.VMEM((slab + 4 * PLANE, C), f32),
            pltpu.VMEM((3 * C, NINE), bf16),
        ],
        place, delta, weight, outer_slab, mib=8,
    )[0]


def near_kernel(parts, out):
    out[...] = jnp.sum(parts[...].astype(f32), axis=0).astype(bf16)


def near_call(parts):
    return call(near_kernel, [(parts.shape[1:], bf16)], [], parts)[0]


def far_kernel(factor, parts, first, second):
    _, split, both, _ = parts.shape
    tall = both // 2
    part = first.shape[0]
    piece = -(-part // split)
    for s in range(split):
        total = jnp.sum(parts[:, s].astype(f32), axis=0) * factor
        rows = min(piece, part - s * piece)
        first[s * piece : s * piece + rows, :] = total[:rows]
        second[s * piece : s * piece + rows, :] = total[tall : tall + rows]


def far_call(parts, part, factor):
    return call(
        functools.partial(far_kernel, factor),
        [((part, C), f32), ((part, C), f32)], [], parts,
    )


def spread(x, axes, count):
    copies = jnp.broadcast_to(x[None], (count,) + x.shape)
    return lax.all_to_all(copies, axes, 0, 0, tiled=True)


def solution(mesh):
    dp, space = mesh.shape["dp"], mesh.shape["space"]
    across = 4
    fine = Mesh(
        mesh.devices.reshape(dp // (2 * across), across, 2, space),
        ("y", "x", "core", "space"),
    )
    chips = dp // 2
    swap = [(0, 1), (1, 0)]
    near = 2 * across
    far = dp // near

    def shifted(x, hops):
        pairs = [((i + hops) % space, i) for i in range(space)]
        return lax.ppermute(x, "space", pairs)

    def whole_patch(x):
        blocks = [((0,), x)]
        up = down = x
        for hops in range(1, space // 2):
            up = shifted(up, 1)
            down = shifted(down, -1)
            blocks += [((hops,), up), ((-hops,), down)]
        return blocks + [((space // 2,), shifted(x, space // 2))]

    def step(image, cotangent, first_weight, second_weight):
        slab = image.shape[1] * PLANE
        cells = slab * space
        part = first_weight.shape[0]
        padded = -(-part // 8) * 8
        piece = -(-part // space)
        chunks = (near, far, 2 * (-(-piece // 8) * 8), C)
        factor = 1.0 / math.sqrt(cells * dp)
        core = lax.axis_index("core")
        place = jnp.stack([lax.axis_index("space"), core]).astype(jnp.int32)

        tall = ((0, padded - part), (0, 0))
        shard = jnp.concatenate([jnp.pad(first_weight, tall), jnp.pad(second_weight, tall)])
        mine = spread(shard, ("y", "x"), chips)
        pair = jnp.concatenate([image.reshape(slab, C), cotangent.reshape(slab, C)])
        blocks = whole_patch(pair)
        theirs = lax.ppermute(mine, "core", swap)
        output, outer_slab, first_delta, grads, w1 = main_call(
            place, blocks, mine, theirs, slab, chunks
        )
        parts = lax.all_to_all(grads, ("x", "core"), 0, 0, tiled=True)
        image_grad = fourth_call(place, first_delta, w1, outer_slab)
        sums = near_call(parts)
        spaced = jnp.broadcast_to(sums[:, None], (far, space) + sums.shape[1:])
        ends = lax.all_to_all(
            spaced.reshape((far * space,) + sums.shape[1:]), ("y", "space"), 0, 0, tiled=True
        )
        first_grad, second_grad = far_call(
            ends.reshape((far, space) + sums.shape[1:]), part, factor
        )
        return (
            output.reshape(image.shape),
            image_grad.reshape(image.shape),
            first_grad,
            second_grad,
        )

    dp_axes = ("y", "x", "core")
    field = P(dp_axes, "space", None, None, None)
    rows = P(dp_axes, None)
    return jax.shard_map(
        step,
        mesh=fine,
        in_specs=(field, field, rows, rows),
        out_specs=(field, field, rows, rows),
        check_vma=False,
    )
```

```python
import functools
import math

import jax
import jax.numpy as jnp
from jax import lax
from jax.experimental import pallas as pl
from jax.experimental.pallas import tpu as pltpu
from jax.sharding import Mesh, PartitionSpec as P


EPSILON = 1e-05
C = 128
H = 8
W = 8
PLANE = H * W
TAPS = 27
NINE = 9 * C
ROWS = TAPS * C
BLOCK = 128
STEP = 16
SPLIT = 8

bf16 = jnp.bfloat16
f32 = jnp.float32


def phi_parts(u):
    cdf = 0.5 * (1.0 + lax.erf(u * 0.7071067811865476))
    return cdf


def slope_of(u, cdf):
    return cdf + u * jnp.exp(-0.5 * u * u) * 0.3989422804014327


def put_w_shifts(value, out, row):
    rows = value.shape[0]
    x = value.reshape(rows // PLANE, H, W, C)
    w_at = lax.broadcasted_iota(jnp.int32, x.shape, 2)
    left = jnp.where(w_at >= 1, pltpu.roll(x, 1, axis=2), 0.0)
    right = jnp.where(w_at <= W - 2, pltpu.roll(x, W - 1, axis=2), 0.0)
    for c, y in enumerate((left, x, right)):
        out[pl.ds(row, rows), c * C : (c + 1) * C] = y.reshape(rows, C).astype(bf16)


def h_down(x):
    return jnp.concatenate([jnp.zeros_like(x[:, :1]), x[:, : H - 1]], axis=1)


def h_up(x):
    return jnp.concatenate([x[:, 1:], jnp.zeros_like(x[:, :1])], axis=1)


def put_h_shifts(value, out, row):
    rows = value.shape[0]
    x = value.reshape(rows // PLANE, H, W, C)
    for b, y in enumerate((h_up(x), x, h_down(x))):
        out[pl.ds(row, rows), b * C : (b + 1) * C] = y.reshape(rows, C).astype(bf16)


def conv_into(acc, source, weight, planes, step, turned=None):
    rows = step * PLANE

    margin = 2 * PLANE

    def clear(i, _):
        at = pl.ds(pl.multiple_of(i * margin, margin), margin)
        acc[at, :] = jnp.zeros((margin, C), f32)
        return 0

    lax.fori_loop(0, (planes + 2) // 2, clear, 0)

    def one(i, _):
        row = pl.multiple_of(i * rows, rows)
        z = jnp.dot(source[pl.ds(row, rows), :], weight[...], preferred_element_type=f32)
        for a in range(3):
            x = [
                z[:, (3 * a + b) * C : (3 * a + b + 1) * C].reshape(step, H, W, C)
                for b in range(3)
            ]
            total = h_down(x[0]) + x[1] + h_up(x[2])
            at = pl.ds(pl.multiple_of(row + (2 - a) * PLANE, PLANE), rows)
            acc[at, :] += total.reshape(rows, C)
        if turned is not None:
            for n in range(rows // C):
                at = pl.multiple_of(row + n * C, C)
                for c in range(3):
                    block = source[pl.ds(at, C), c * C : (c + 1) * C]
                    turned[c * C : (c + 1) * C, pl.ds(at, C)] = block.T
        return 0

    lax.fori_loop(0, planes // step, one, 0)


def by_taps(flat, weight):
    for k in range(TAPS):
        c, ab = k % 3, k // 3
        weight[c * C : (c + 1) * C, ab * C : (ab + 1) * C] = flat[
            k * C : (k + 1) * C, :
        ].astype(bf16)


def reverse_into(weight, out):
    for k in range(TAPS):
        c, ab = k % 3, k // 3
        block = weight[(2 - c) * C : (3 - c) * C, (8 - ab) * C : (9 - ab) * C]
        out[c * C : (c + 1) * C, ab * C : (ab + 1) * C] = block.T


def assemble(core, mine, theirs, flat, weight):
    across, chips = mine.shape[0], mine.shape[0] * mine.shape[1]
    part = ROWS // (2 * chips)
    mine_first = core == 0
    for y in range(chips):
        one = mine[y % across, y // across].astype(f32)
        two = theirs[y % across, y // across].astype(f32)
        even = jnp.where(mine_first, one, two)[:part]
        odd = jnp.where(mine_first, two, one)[:part]
        flat[2 * y * part : (2 * y + 1) * part, :] = even
        flat[(2 * y + 1) * part : (2 * y + 2) * part, :] = odd
    by_taps(flat, weight)


def row_sum(x):
    return jnp.sum(x, axis=0, keepdims=True)


def grad_into(turned, delta, cells, flat, out, place, top):
    def shifted(a, first, last):
        row = (2 - a) * PLANE
        return delta[row : row + cells, first * C : last * C]

    jobs = [([(a, 0), (a, 1)], lambda a=a: shifted(a, 0, 2)) for a in range(3)]
    jobs.append(
        ([(0, 2), (1, 2)], lambda: jnp.concatenate([shifted(0, 2, 3), shifted(1, 2, 3)], axis=1))
    )
    jobs.append(([(2, 2)], lambda: shifted(2, 2, 3)))
    for taps, side in jobs:
        total = jnp.dot(turned[...], side(), preferred_element_type=f32)
        for n, (a, b) in enumerate(taps):
            for c in range(3):
                row = (9 * a + 3 * b + c) * C
                flat[row : row + C, :] = total[c * C : (c + 1) * C, n * C : (n + 1) * C]
    near, far, tall, _ = out.shape
    part = ROWS // (near * far)
    tall = tall // 2
    base = place[0] * (-(-part // SPLIT))
    for j in range(near * far):
        chunk = flat[pl.ds(j * part + base, tall), :].astype(bf16)
        out[j % near, j // near, top : top + tall, :] = chunk


def blocks_of(cells, body, init, rows=BLOCK):
    def one(i, carry):
        return body(i, pl.multiple_of(i * rows, rows), carry)

    return lax.fori_loop(0, cells // rows, one, init)


def statistics(conv, cells):
    zero = jnp.zeros((1, C), f32)

    def one(i, row, sums):
        acc = conv[pl.ds(row + PLANE, 4 * BLOCK), :]
        return (sums[0] + row_sum(acc), sums[1] + row_sum(acc * acc))

    total, square = blocks_of(cells, one, (zero, zero), 4 * BLOCK)
    average = total / cells
    return average, lax.rsqrt(square / cells - average * average + EPSILON)


def main_kernel(offsets, place, *refs):
    blocks, refs = refs[: len(offsets)], refs[len(offsets) :]
    (
        mine, theirs,
        output, outer_out, delta_out, grads_out, weight_out,
        image, cotangent, first_delta, outer_slab, grads,
        mine1, theirs1, mine2, theirs2, weight1, weight2, turned_weight,
        image_three, three, delta_three, image_turned, turned, normed, conv, outer, flat,
        image_sem, other_sem, weight_sem, out_sem,
    ) = refs
    cells = image.shape[0]
    planes = cells // PLANE
    slab = output.shape[0]
    count = cells // slab
    padded = mine1.shape[2]
    zero = jnp.zeros((1, C), f32)
    copy = pltpu.make_async_copy
    fields = ([], [])
    for n, ((offset, index), block) in enumerate(zip(offsets, blocks)):
        owner = lax.rem(place[0] + (offset + count), count)
        at = pl.ds(pl.multiple_of(owner * slab, slab), slab)
        row = 2 * index * slab
        fields[0].append(copy(block.at[row : row + slab], image.at[at], image_sem.at[n]))
        fields[1].append(
            copy(block.at[row + slab : row + 2 * slab], cotangent.at[at], other_sem.at[n])
        )
    weights = [
        copy(source.at[:, :, half * padded : (half + 1) * padded], target, weight_sem.at[n])
        for n, (source, half, target) in enumerate(
            ((mine, 0, mine1), (theirs, 0, theirs1), (mine, 1, mine2), (theirs, 1, theirs2))
        )
    ]
    for c in fields[0] + weights + fields[1]:
        c.start()
    edge = jnp.zeros((PLANE, 3 * C), bf16)
    delta_three[0:PLANE, :] = edge
    delta_three[cells + PLANE : cells + 2 * PLANE, :] = edge
    for c in fields[0]:
        c.wait()

    def shift_image(i, row, _):
        put_w_shifts(image[pl.ds(row, BLOCK), :].astype(f32), image_three, row)
        return 0

    blocks_of(cells, shift_image, 0)
    for c in weights[:2]:
        c.wait()
    assemble(place[1], mine1, theirs1, flat, weight1)
    weight_copy = copy(weight1, weight_out, out_sem.at[0])
    weight_copy.start()
    conv_into(conv, image_three, weight1, planes, STEP, image_turned)
    average1, inverse1 = statistics(conv, cells)

    def norm_one(i, row, _):
        u = (conv[pl.ds(row + PLANE, BLOCK), :] - average1) * inverse1
        normed[pl.ds(row, BLOCK), :] = u
        put_w_shifts(u * phi_parts(u), three, row)
        return 0

    blocks_of(cells, norm_one, 0)
    for c in weights[2:]:
        c.wait()
    assemble(place[1], mine2, theirs2, flat, weight2)
    conv_into(conv, three, weight2, planes, STEP, turned)
    average, inverse = statistics(conv, cells)
    for c in fields[1]:
        c.wait()
    parts = slab // BLOCK

    def norm_two(i, row, sums):
        at = pl.ds(row, BLOCK)
        n = (conv[pl.ds(row + PLANE, BLOCK), :] - average) * inverse
        conv[pl.ds(row + PLANE, BLOCK), :] = n
        u = image[at, :].astype(f32) + n
        cdf = phi_parts(u)
        grad = cotangent[at, :].astype(f32) * slope_of(u, cdf)
        outer[at, :] = grad

        @pl.when(lax.div(i, parts) == place[0])
        def _():
            inner = pl.ds(pl.multiple_of(lax.rem(i, parts) * BLOCK, BLOCK), BLOCK)
            output[inner, :] = (u * cdf).astype(bf16)
            outer_slab[inner, :] = grad

        return (sums[0] + row_sum(grad), sums[1] + row_sum(grad * n))

    plain, paired = blocks_of(cells, norm_two, (zero, zero))
    outer_copy = copy(outer_slab, outer_out, out_sem.at[1])
    outer_copy.start()
    plain = plain / cells
    paired = paired / cells

    def back_two(i, row, _):
        n = conv[pl.ds(row + PLANE, BLOCK), :]
        value = inverse * (outer[pl.ds(row, BLOCK), :] - plain - n * paired)
        put_w_shifts(value, three, row)
        put_h_shifts(value, delta_three, row + PLANE)
        return 0

    blocks_of(cells, back_two, 0)
    half = grads.shape[2] // 2
    grad_into(turned, delta_three, cells, flat, grads, place, half)

    reverse_into(weight2, turned_weight)
    conv_into(conv, three, turned_weight, planes, STEP)

    def inner_grad(i, row, sums):
        u = normed[pl.ds(row, BLOCK), :]
        grad = conv[pl.ds(row + PLANE, BLOCK), :] * slope_of(u, phi_parts(u))
        conv[pl.ds(row + PLANE, BLOCK), :] = grad
        return (sums[0] + row_sum(grad), sums[1] + row_sum(grad * u))

    plain1, paired1 = blocks_of(cells, inner_grad, (zero, zero))
    plain1 = plain1 / cells
    paired1 = paired1 / cells

    def back_one(i, row, _):
        at = pl.ds(row, BLOCK)
        grad = conv[pl.ds(row + PLANE, BLOCK), :]
        value = inverse1 * (grad - plain1 - normed[at, :] * paired1)
        first_delta[at, :] = value.astype(bf16)
        put_h_shifts(value, delta_three, row + PLANE)
        return 0

    blocks_of(cells, back_one, 0)
    delta_copy = copy(first_delta, delta_out, out_sem.at[2])
    delta_copy.start()
    grad_into(image_turned, delta_three, cells, flat, grads, place, 0)
    grads_copy = copy(grads, grads_out, out_sem.at[3])
    grads_copy.start()
    for c in (weight_copy, outer_copy, delta_copy, grads_copy):
        c.wait()


def fourth_kernel(place, delta, weight, outer_slab, grad, three, conv, turned_weight):
    slab = grad.shape[0]
    planes = slab // PLANE
    last = delta.shape[0] // PLANE
    reverse_into(weight, turned_weight)
    base = place[0] * planes
    for p in range(planes + 2):
        d = base + (p - 1)
        inside = jnp.logical_and(d >= 0, d < last)
        at = pl.multiple_of(jnp.clip(d, 0, last - 1) * PLANE, PLANE)
        x = delta[pl.ds(at, PLANE), :].astype(f32)
        put_w_shifts(jnp.where(inside, x, 0.0), three, p * PLANE)
    conv_into(conv, three, turned_weight, planes + 2, planes + 2)
    total = conv[2 * PLANE : 2 * PLANE + slab, :]
    grad[...] = (outer_slab[...] + total).astype(bf16)


SMEM = pl.BlockSpec(memory_space=pltpu.SMEM)
VMEM = pl.BlockSpec(memory_space=pltpu.VMEM)
HBM = pl.BlockSpec(memory_space=pltpu.HBM)


def call(kernel, outs, scratch, *args, mib=4, far_in=(), far_out=()):
    specs = [
        HBM if n in far_in else SMEM if a.dtype == jnp.int32 else VMEM
        for n, a in enumerate(args)
    ]
    args = [
        pltpu.with_memory_space_constraint(a, pltpu.HBM) if n in far_in else a
        for n, a in enumerate(args)
    ]
    return pl.pallas_call(
        kernel,
        out_shape=tuple(jax.ShapeDtypeStruct(s, d) for s, d in outs),
        in_specs=specs,
        out_specs=tuple(HBM if n in far_out else VMEM for n in range(len(outs))),
        scratch_shapes=scratch,
        compiler_params=pltpu.CompilerParams(vmem_limit_bytes=mib * 1024 * 1024),
    )(*args)


def main_call(place, blocks, mine, theirs, slab, chunks):
    count = sum(len(offsets) for offsets, _ in blocks)
    cells = slab * count
    offsets = [(o, n) for many, _ in blocks for n, o in enumerate(many)]
    arrays = [array for many, array in blocks for _ in many]
    field = (cells, C)
    half = mine.shape[:2] + (mine.shape[2] // 2, C)
    local = pltpu.VMEM
    signal = pltpu.SemaphoreType.DMA
    return call(
        functools.partial(main_kernel, offsets),
        [
            ((slab, C), bf16), ((slab, C), f32), (field, bf16), (chunks, bf16),
            ((3 * C, NINE), bf16),
        ],
        [local(field, bf16)] * 3
        + [local((slab, C), f32), local(chunks, bf16)]
        + [local(half, bf16)] * 4
        + [local((3 * C, NINE), bf16)] * 3
        + [
            local((cells, 3 * C), bf16), local((cells, 3 * C), bf16),
            local((cells + 2 * PLANE, 3 * C), bf16),
            local((3 * C, cells), bf16), local((3 * C, cells), bf16),
            local(field, f32), local((cells + 2 * PLANE, C), f32), local(field, f32),
            local((ROWS + 8, C), f32),
            signal((count,)), signal((count,)), signal((4,)), signal((4,)),
        ],
        place, *arrays, mine, theirs,
        mib=32, far_in=range(1, count + 3), far_out=(1, 2, 3, 4),
    )


def fourth_call(place, delta, weight, outer_slab):
    slab = outer_slab.shape[0]
    return call(
        fourth_kernel,
        [((slab, C), bf16)],
        [
            pltpu.VMEM((slab + 2 * PLANE, 3 * C), bf16),
            pltpu.VMEM((slab + 4 * PLANE, C), f32),
            pltpu.VMEM((3 * C, NINE), bf16),
        ],
        place, delta, weight, outer_slab, mib=8,
    )[0]


def near_kernel(parts, out):
    out[...] = jnp.sum(parts[...].astype(f32), axis=0).astype(bf16)


def near_call(parts):
    return call(near_kernel, [(parts.shape[1:], bf16)], [], parts)[0]


def far_kernel(factor, parts, first, second):
    _, split, both, _ = parts.shape
    tall = both // 2
    part = first.shape[0]
    piece = -(-part // split)
    for s in range(split):
        total = jnp.sum(parts[:, s].astype(f32), axis=0) * factor
        rows = min(piece, part - s * piece)
        first[s * piece : s * piece + rows, :] = total[:rows]
        second[s * piece : s * piece + rows, :] = total[tall : tall + rows]


def far_call(parts, part, factor):
    return call(
        functools.partial(far_kernel, factor),
        [((part, C), f32), ((part, C), f32)], [], parts,
    )


def spread(x, axes, count):
    copies = jnp.broadcast_to(x[None], (count,) + x.shape)
    return lax.all_to_all(copies, axes, 0, 0, tiled=True)


def solution(mesh):
    dp, space = mesh.shape["dp"], mesh.shape["space"]
    across = 4
    fine = Mesh(
        mesh.devices.reshape(dp // (2 * across), across, 2, space),
        ("y", "x", "core", "space"),
    )
    swap = [(0, 1), (1, 0)]
    near = 2 * across
    far = dp // near

    def shifted(x, hops):
        pairs = [((i + hops) % space, i) for i in range(space)]
        return lax.ppermute(x, "space", pairs)

    def whole_patch(x):
        blocks = [((0,), x)]
        up = down = x
        for hops in range(1, space // 2):
            up = shifted(up, 1)
            down = shifted(down, -1)
            blocks += [((hops,), up), ((-hops,), down)]
        return blocks + [((space // 2,), shifted(x, space // 2))]

    def step(image, cotangent, first_weight, second_weight):
        slab = image.shape[1] * PLANE
        cells = slab * space
        part = first_weight.shape[0]
        padded = -(-part // 8) * 8
        piece = -(-part // space)
        chunks = (near, far, 2 * (-(-piece // 8) * 8), C)
        factor = 1.0 / math.sqrt(cells * dp)
        core = lax.axis_index("core")
        place = jnp.stack([lax.axis_index("space"), core]).astype(jnp.int32)

        tall = ((0, padded - part), (0, 0))
        shard = jnp.concatenate([jnp.pad(first_weight, tall), jnp.pad(second_weight, tall)])
        column = spread(shard, "y", far)
        mine = spread(column, "x", across)
        pair = jnp.concatenate([image.reshape(slab, C), cotangent.reshape(slab, C)])
        blocks = whole_patch(pair)
        theirs = lax.ppermute(mine, "core", swap)
        output, outer_slab, first_delta, grads, w1 = main_call(
            place, blocks, mine, theirs, slab, chunks
        )
        parts = lax.all_to_all(grads, ("x", "core"), 0, 0, tiled=True)
        image_grad = fourth_call(place, first_delta, w1, outer_slab)
        sums = near_call(parts)
        spaced = jnp.broadcast_to(sums[:, None], (far, space) + sums.shape[1:])
        ends = lax.all_to_all(
            spaced.reshape((far * space,) + sums.shape[1:]), ("y", "space"), 0, 0, tiled=True
        )
        first_grad, second_grad = far_call(
            ends.reshape((far, space) + sums.shape[1:]), part, factor
        )
        return (
            output.reshape(image.shape),
            image_grad.reshape(image.shape),
            first_grad,
            second_grad,
        )

    dp_axes = ("y", "x", "core")
    field = P(dp_axes, "space", None, None, None)
    rows = P(dp_axes, None)
    return jax.shard_map(
        step,
        mesh=fine,
        in_specs=(field, field, rows, rows),
        out_specs=(field, field, rows, rows),
        check_vma=False,
    )
```

```python
import functools
import math

import jax
import jax.numpy as jnp
from jax import lax
from jax.experimental import pallas as pl
from jax.experimental.pallas import tpu as pltpu
from jax.sharding import Mesh, PartitionSpec as P


EPSILON = 1e-05
C = 128
H = 8
W = 8
PLANE = H * W
TAPS = 27
NINE = 9 * C
ROWS = TAPS * C
BLOCK = 128
STEP = 16
SPLIT = 8

bf16 = jnp.bfloat16
f32 = jnp.float32


def phi_parts(u):
    cdf = 0.5 * (1.0 + lax.erf(u * 0.7071067811865476))
    return cdf


def slope_of(u, cdf):
    return cdf + u * jnp.exp(-0.5 * u * u) * 0.3989422804014327


def put_w_shifts(value, out, row):
    rows = value.shape[0]
    x = value.reshape(rows // PLANE, H, W, C)
    w_at = lax.broadcasted_iota(jnp.int32, x.shape, 2)
    left = jnp.where(w_at >= 1, pltpu.roll(x, 1, axis=2), 0.0)
    right = jnp.where(w_at <= W - 2, pltpu.roll(x, W - 1, axis=2), 0.0)
    for c, y in enumerate((left, x, right)):
        out[pl.ds(row, rows), c * C : (c + 1) * C] = y.reshape(rows, C).astype(bf16)


def h_down(x):
    return jnp.concatenate([jnp.zeros_like(x[:, :1]), x[:, : H - 1]], axis=1)


def h_up(x):
    return jnp.concatenate([x[:, 1:], jnp.zeros_like(x[:, :1])], axis=1)


def put_h_shifts(value, out, row):
    rows = value.shape[0]
    x = value.reshape(rows // PLANE, H, W, C)
    for b, y in enumerate((h_up(x), x, h_down(x))):
        out[pl.ds(row, rows), b * C : (b + 1) * C] = y.reshape(rows, C).astype(bf16)


def conv_into(acc, source, weight, planes, step, turned=None, prepare=None, beside=None):
    rows = step * PLANE
    margin = 2 * PLANE

    def clear(i, _):
        at = pl.ds(pl.multiple_of(i * margin, margin), margin)
        acc[at, :] = jnp.zeros((margin, C), f32)
        return 0

    lax.fori_loop(0, (planes + 2) // 2, clear, 0)
    prepare = prepare or (lambda row: None)
    prepare(0)
    for row in range(0, planes * PLANE, rows):
        if row + rows < planes * PLANE:
            prepare(row + rows)
        elif beside is not None:
            beside()
        z = jnp.dot(source[row : row + rows, :], weight[...], preferred_element_type=f32)
        for a in range(3):
            x = [
                z[:, (3 * a + b) * C : (3 * a + b + 1) * C].reshape(step, H, W, C)
                for b in range(3)
            ]
            total = h_down(x[0]) + x[1] + h_up(x[2])
            top = row + (2 - a) * PLANE
            acc[top : top + rows, :] += total.reshape(rows, C)
        if turned is not None:
            for at in range(row, row + rows, C):
                for c in range(3):
                    block = source[at : at + C, c * C : (c + 1) * C]
                    turned[c * C : (c + 1) * C, at : at + C] = block.T


def by_taps(flat, weight):
    for k in range(TAPS):
        c, ab = k % 3, k // 3
        weight[c * C : (c + 1) * C, ab * C : (ab + 1) * C] = flat[
            k * C : (k + 1) * C, :
        ].astype(bf16)


def reverse_into(weight, out):
    for k in range(TAPS):
        c, ab = k % 3, k // 3
        block = weight[(2 - c) * C : (3 - c) * C, (8 - ab) * C : (9 - ab) * C]
        out[c * C : (c + 1) * C, ab * C : (ab + 1) * C] = block.T


def assemble(core, mine, theirs, flat, weight):
    chips = mine.shape[0]
    part = ROWS // (2 * chips)
    mine_first = core == 0
    for y in range(chips):
        one = mine[y].astype(f32)
        two = theirs[y].astype(f32)
        even = jnp.where(mine_first, one, two)[:part]
        odd = jnp.where(mine_first, two, one)[:part]
        flat[2 * y * part : (2 * y + 1) * part, :] = even
        flat[(2 * y + 1) * part : (2 * y + 2) * part, :] = odd
    by_taps(flat, weight)


def row_sum(x):
    return jnp.sum(x, axis=0, keepdims=True)


def grad_into(turned, delta, cells, flat, out, place, top):
    def shifted(a, first, last):
        row = (2 - a) * PLANE
        return delta[row : row + cells, first * C : last * C]

    jobs = [([(a, 0), (a, 1)], lambda a=a: shifted(a, 0, 2)) for a in range(3)]
    jobs.append(
        ([(0, 2), (1, 2)], lambda: jnp.concatenate([shifted(0, 2, 3), shifted(1, 2, 3)], axis=1))
    )
    jobs.append(([(2, 2)], lambda: shifted(2, 2, 3)))
    for taps, side in jobs:
        total = jnp.dot(turned[...], side(), preferred_element_type=f32)
        for n, (a, b) in enumerate(taps):
            for c in range(3):
                row = (9 * a + 3 * b + c) * C
                flat[row : row + C, :] = total[c * C : (c + 1) * C, n * C : (n + 1) * C]
    near, far, tall, _ = out.shape
    part = ROWS // (near * far)
    tall = tall // 2
    base = place[0] * (-(-part // SPLIT))
    for j in range(near * far):
        chunk = flat[pl.ds(j * part + base, tall), :].astype(bf16)
        out[j % near, j // near, top : top + tall, :] = chunk


def blocks_of(cells, body, init, rows=BLOCK):
    def one(i, carry):
        return body(i, pl.multiple_of(i * rows, rows), carry)

    return lax.fori_loop(0, cells // rows, one, init)


def statistics(conv, cells):
    zero = jnp.zeros((1, C), f32)

    def one(i, row, sums):
        acc = conv[pl.ds(row + PLANE, 4 * BLOCK), :]
        return (sums[0] + row_sum(acc), sums[1] + row_sum(acc * acc))

    total, square = blocks_of(cells, one, (zero, zero), 4 * BLOCK)
    average = total / cells
    return average, lax.rsqrt(square / cells - average * average + EPSILON)


def main_kernel(offsets, place, *refs):
    blocks, refs = refs[: len(offsets)], refs[len(offsets) :]
    (
        mine, theirs,
        output, outer_out, delta_out, grads_out, weight_out,
        image, cotangent, first_delta, outer_slab, grads,
        mine1, theirs1, mine2, theirs2, weight1, weight2, turned_weight,
        image_three, three, delta_three, image_turned, turned, normed, conv, conv2, outer, flat,
        image_sem, other_sem, weight_sem, out_sem,
    ) = refs
    cells = image.shape[0]
    planes = cells // PLANE
    slab = output.shape[0]
    count = cells // slab
    padded = mine1.shape[1]
    zero = jnp.zeros((1, C), f32)
    copy = pltpu.make_async_copy
    fields = ([], [])
    for n, ((offset, index), block) in enumerate(zip(offsets, blocks)):
        owner = lax.rem(place[0] + (offset + count), count)
        at = pl.ds(pl.multiple_of(owner * slab, slab), slab)
        row = 2 * index * slab
        fields[0].append(copy(block.at[row : row + slab], image.at[at], image_sem.at[n]))
        fields[1].append(
            copy(block.at[row + slab : row + 2 * slab], cotangent.at[at], other_sem.at[n])
        )
    weights = [
        copy(source.at[:, half * padded : (half + 1) * padded], target, weight_sem.at[n])
        for n, (source, half, target) in enumerate(
            ((mine, 0, mine1), (theirs, 0, theirs1), (mine, 1, mine2), (theirs, 1, theirs2))
        )
    ]
    for c in fields[0] + weights + fields[1]:
        c.start()
    edge = jnp.zeros((PLANE, 3 * C), bf16)
    delta_three[0:PLANE, :] = edge
    delta_three[cells + PLANE : cells + 2 * PLANE, :] = edge
    for c in fields[0]:
        c.wait()

    def each(row, body):
        for n in range(row, row + STEP * PLANE, BLOCK):
            body(n)

    def shift_image(n):
        put_w_shifts(image[n : n + BLOCK, :].astype(f32), image_three, n)

    for c in weights:
        c.wait()
    assemble(place[1], mine1, theirs1, flat, weight1)
    weight_copy = copy(weight1, weight_out, out_sem.at[0])
    weight_copy.start()
    conv_into(
        conv, image_three, weight1, planes, STEP, image_turned,
        lambda row: each(row, shift_image),
        lambda: assemble(place[1], mine2, theirs2, flat, weight2),
    )
    average1, inverse1 = statistics(conv, cells)

    def norm_one(n):
        u = (conv[n + PLANE : n + PLANE + BLOCK, :] - average1) * inverse1
        normed[n : n + BLOCK, :] = u
        put_w_shifts(u * phi_parts(u), three, n)

    conv_into(
        conv2, three, weight2, planes, STEP, turned,
        lambda row: each(row, norm_one),
        lambda: reverse_into(weight2, turned_weight),
    )
    average, inverse = statistics(conv2, cells)
    for c in fields[1]:
        c.wait()
    parts = slab // BLOCK

    def norm_two(i, row, sums):
        at = pl.ds(row, BLOCK)
        n = (conv2[pl.ds(row + PLANE, BLOCK), :] - average) * inverse
        conv2[pl.ds(row + PLANE, BLOCK), :] = n
        u = image[at, :].astype(f32) + n
        cdf = phi_parts(u)
        grad = cotangent[at, :].astype(f32) * slope_of(u, cdf)
        outer[at, :] = grad

        @pl.when(lax.div(i, parts) == place[0])
        def _():
            inner = pl.ds(pl.multiple_of(lax.rem(i, parts) * BLOCK, BLOCK), BLOCK)
            output[inner, :] = (u * cdf).astype(bf16)
            outer_slab[inner, :] = grad

        return (sums[0] + row_sum(grad), sums[1] + row_sum(grad * n))

    plain, paired = blocks_of(cells, norm_two, (zero, zero))
    outer_copy = copy(outer_slab, outer_out, out_sem.at[1])
    outer_copy.start()
    plain = plain / cells
    paired = paired / cells

    def back_two(i, row, _):
        n = conv2[pl.ds(row + PLANE, BLOCK), :]
        value = inverse * (outer[pl.ds(row, BLOCK), :] - plain - n * paired)
        put_w_shifts(value, three, row)
        put_h_shifts(value, delta_three, row + PLANE)
        return 0

    blocks_of(cells, back_two, 0)
    half = grads.shape[2] // 2
    grad_into(turned, delta_three, cells, flat, grads, place, half)

    conv_into(conv, three, turned_weight, planes, STEP)

    def inner_grad(i, row, sums):
        u = normed[pl.ds(row, BLOCK), :]
        grad = conv[pl.ds(row + PLANE, BLOCK), :] * slope_of(u, phi_parts(u))
        conv[pl.ds(row + PLANE, BLOCK), :] = grad
        return (sums[0] + row_sum(grad), sums[1] + row_sum(grad * u))

    plain1, paired1 = blocks_of(cells, inner_grad, (zero, zero))
    plain1 = plain1 / cells
    paired1 = paired1 / cells

    def back_one(i, row, _):
        at = pl.ds(row, BLOCK)
        grad = conv[pl.ds(row + PLANE, BLOCK), :]
        value = inverse1 * (grad - plain1 - normed[at, :] * paired1)
        first_delta[at, :] = value.astype(bf16)
        put_h_shifts(value, delta_three, row + PLANE)
        return 0

    blocks_of(cells, back_one, 0)
    delta_copy = copy(first_delta, delta_out, out_sem.at[2])
    delta_copy.start()
    grad_into(image_turned, delta_three, cells, flat, grads, place, 0)
    grads_copy = copy(grads, grads_out, out_sem.at[3])
    grads_copy.start()
    for c in (weight_copy, outer_copy, delta_copy, grads_copy):
        c.wait()


def fourth_kernel(place, delta, weight, outer_slab, grad, three, conv, turned_weight):
    slab = grad.shape[0]
    planes = slab // PLANE
    last = delta.shape[0] // PLANE
    reverse_into(weight, turned_weight)
    base = place[0] * planes
    for p in range(planes + 2):
        d = base + (p - 1)
        inside = jnp.logical_and(d >= 0, d < last)
        at = pl.multiple_of(jnp.clip(d, 0, last - 1) * PLANE, PLANE)
        x = delta[pl.ds(at, PLANE), :].astype(f32)
        put_w_shifts(jnp.where(inside, x, 0.0), three, p * PLANE)
    conv_into(conv, three, turned_weight, planes + 2, planes + 2)
    total = conv[2 * PLANE : 2 * PLANE + slab, :]
    grad[...] = (outer_slab[...] + total).astype(bf16)


SMEM = pl.BlockSpec(memory_space=pltpu.SMEM)
VMEM = pl.BlockSpec(memory_space=pltpu.VMEM)
HBM = pl.BlockSpec(memory_space=pltpu.HBM)


def call(kernel, outs, scratch, *args, mib=4, far_in=(), far_out=()):
    specs = [
        HBM if n in far_in else SMEM if a.dtype == jnp.int32 else VMEM
        for n, a in enumerate(args)
    ]
    args = [
        pltpu.with_memory_space_constraint(a, pltpu.HBM) if n in far_in else a
        for n, a in enumerate(args)
    ]
    return pl.pallas_call(
        kernel,
        out_shape=tuple(jax.ShapeDtypeStruct(s, d) for s, d in outs),
        in_specs=specs,
        out_specs=tuple(HBM if n in far_out else VMEM for n in range(len(outs))),
        scratch_shapes=scratch,
        compiler_params=pltpu.CompilerParams(vmem_limit_bytes=mib * 1024 * 1024),
    )(*args)


def main_call(place, blocks, mine, theirs, slab, chunks):
    count = sum(len(offsets) for offsets, _ in blocks)
    cells = slab * count
    offsets = [(o, n) for many, _ in blocks for n, o in enumerate(many)]
    arrays = [array for many, array in blocks for _ in many]
    field = (cells, C)
    half = (mine.shape[0], mine.shape[1] // 2, C)
    local = pltpu.VMEM
    signal = pltpu.SemaphoreType.DMA
    return call(
        functools.partial(main_kernel, offsets),
        [
            ((slab, C), bf16), ((slab, C), f32), (field, bf16), (chunks, bf16),
            ((3 * C, NINE), bf16),
        ],
        [local(field, bf16)] * 3
        + [local((slab, C), f32), local(chunks, bf16)]
        + [local(half, bf16)] * 4
        + [local((3 * C, NINE), bf16)] * 3
        + [
            local((cells, 3 * C), bf16), local((cells, 3 * C), bf16),
            local((cells + 2 * PLANE, 3 * C), bf16),
            local((3 * C, cells), bf16), local((3 * C, cells), bf16),
            local(field, f32), local((cells + 2 * PLANE, C), f32),
            local((cells + 2 * PLANE, C), f32), local(field, f32),
            local((ROWS + 8, C), f32),
            signal((count,)), signal((count,)), signal((4,)), signal((4,)),
        ],
        place, *arrays, mine, theirs,
        mib=32, far_in=range(1, count + 3), far_out=(1, 2, 3, 4),
    )


def fourth_call(place, delta, weight, outer_slab):
    slab = outer_slab.shape[0]
    return call(
        fourth_kernel,
        [((slab, C), bf16)],
        [
            pltpu.VMEM((slab + 2 * PLANE, 3 * C), bf16),
            pltpu.VMEM((slab + 4 * PLANE, C), f32),
            pltpu.VMEM((3 * C, NINE), bf16),
        ],
        place, delta, weight, outer_slab, mib=8,
    )[0]


def near_kernel(parts, out):
    out[...] = jnp.sum(parts[...].astype(f32), axis=0).astype(bf16)


def near_call(parts):
    return call(near_kernel, [(parts.shape[1:], bf16)], [], parts)[0]


def far_kernel(factor, parts, first, second):
    _, split, both, _ = parts.shape
    tall = both // 2
    part = first.shape[0]
    piece = -(-part // split)
    for s in range(split):
        total = jnp.sum(parts[:, s].astype(f32), axis=0) * factor
        rows = min(piece, part - s * piece)
        first[s * piece : s * piece + rows, :] = total[:rows]
        second[s * piece : s * piece + rows, :] = total[tall : tall + rows]


def far_call(parts, part, factor):
    return call(
        functools.partial(far_kernel, factor),
        [((part, C), f32), ((part, C), f32)], [], parts,
    )


def spread(x, axes, count):
    copies = jnp.broadcast_to(x[None], (count,) + x.shape)
    return lax.all_to_all(copies, axes, 0, 0, tiled=True)


def solution(mesh):
    dp, space = mesh.shape["dp"], mesh.shape["space"]
    across = 4
    fine = Mesh(
        mesh.devices.reshape(dp // (2 * across), across, 2, space),
        ("y", "x", "core", "space"),
    )
    swap = [(0, 1), (1, 0)]
    near = 2 * across
    far = dp // near

    def shifted(x, hops):
        pairs = [((i + hops) % space, i) for i in range(space)]
        return lax.ppermute(x, "space", pairs)

    def whole_patch(x):
        blocks = [((0,), x)]
        up = down = x
        for hops in range(1, space // 2):
            up = shifted(up, 1)
            down = shifted(down, -1)
            blocks += [((hops,), up), ((-hops,), down)]
        return blocks + [((space // 2,), shifted(x, space // 2))]

    def step(image, cotangent, first_weight, second_weight):
        slab = image.shape[1] * PLANE
        cells = slab * space
        part = first_weight.shape[0]
        padded = -(-part // 8) * 8
        piece = -(-part // space)
        chunks = (near, far, 2 * (-(-piece // 8) * 8), C)
        factor = 1.0 / math.sqrt(cells * dp)
        core = lax.axis_index("core")
        place = jnp.stack([lax.axis_index("space"), core]).astype(jnp.int32)

        tall = ((0, padded - part), (0, 0))
        shard = jnp.concatenate([jnp.pad(first_weight, tall), jnp.pad(second_weight, tall)])
        mine = spread(shard, ("y", "x"), far * across)
        pair = jnp.concatenate([image.reshape(slab, C), cotangent.reshape(slab, C)])
        blocks = whole_patch(pair)
        theirs = lax.ppermute(mine, "core", swap)
        output, outer_slab, first_delta, grads, w1 = main_call(
            place, blocks, mine, theirs, slab, chunks
        )
        parts = lax.all_to_all(grads, ("x", "core"), 0, 0, tiled=True)
        image_grad = fourth_call(place, first_delta, w1, outer_slab)
        sums = near_call(parts)
        spaced = jnp.broadcast_to(sums[:, None], (far, space) + sums.shape[1:])
        ends = lax.all_to_all(
            spaced.reshape((far * space,) + sums.shape[1:]), ("y", "space"), 0, 0, tiled=True
        )
        first_grad, second_grad = far_call(
            ends.reshape((far, space) + sums.shape[1:]), part, factor
        )
        return (
            output.reshape(image.shape),
            image_grad.reshape(image.shape),
            first_grad,
            second_grad,
        )

    dp_axes = ("y", "x", "core")
    field = P(dp_axes, "space", None, None, None)
    rows = P(dp_axes, None)
    return jax.shard_map(
        step,
        mesh=fine,
        in_specs=(field, field, rows, rows),
        out_specs=(field, field, rows, rows),
        check_vma=False,
    )
```

```python
import functools
import math

import jax
import jax.numpy as jnp
from jax import lax
from jax.experimental import pallas as pl
from jax.experimental.pallas import tpu as pltpu
from jax.sharding import Mesh, PartitionSpec as P


EPSILON = 1e-05
C = 128
H = 8
W = 8
PLANE = H * W
TAPS = 27
NINE = 9 * C
ROWS = TAPS * C
BLOCK = 128
STEP = 16
SPLIT = 8

bf16 = jnp.bfloat16
f32 = jnp.float32


def phi_parts(u):
    cdf = 0.5 * (1.0 + lax.erf(u * 0.7071067811865476))
    return cdf


def slope_of(u, cdf):
    return cdf + u * jnp.exp(-0.5 * u * u) * 0.3989422804014327


def put_w_shifts(value, out, row):
    rows = value.shape[0]
    x = value.reshape(rows // PLANE, H, W, C)
    w_at = lax.broadcasted_iota(jnp.int32, x.shape, 2)
    left = jnp.where(w_at >= 1, pltpu.roll(x, 1, axis=2), 0.0)
    right = jnp.where(w_at <= W - 2, pltpu.roll(x, W - 1, axis=2), 0.0)
    for c, y in enumerate((left, x, right)):
        out[pl.ds(row, rows), c * C : (c + 1) * C] = y.reshape(rows, C).astype(bf16)


def h_down(x):
    return jnp.concatenate([jnp.zeros_like(x[:, :1]), x[:, : H - 1]], axis=1)


def h_up(x):
    return jnp.concatenate([x[:, 1:], jnp.zeros_like(x[:, :1])], axis=1)


def put_h_shifts(value, out, row):
    rows = value.shape[0]
    x = value.reshape(rows // PLANE, H, W, C)
    for b, y in enumerate((h_up(x), x, h_down(x))):
        out[pl.ds(row, rows), b * C : (b + 1) * C] = y.reshape(rows, C).astype(bf16)


def conv_into(acc, source, weight, planes, step, turned=None, prepare=None, beside=None):
    rows = step * PLANE
    margin = 2 * PLANE

    def clear(i, _):
        at = pl.ds(pl.multiple_of(i * margin, margin), margin)
        acc[at, :] = jnp.zeros((margin, C), f32)
        return 0

    lax.fori_loop(0, (planes + 2) // 2, clear, 0)
    prepare = prepare or (lambda row: None)
    prepare(0)
    for row in range(0, planes * PLANE, rows):
        if row + rows < planes * PLANE:
            prepare(row + rows)
        elif beside is not None:
            beside()
        z = jnp.dot(source[row : row + rows, :], weight[...], preferred_element_type=f32)
        for a in range(3):
            x = [
                z[:, (3 * a + b) * C : (3 * a + b + 1) * C].reshape(step, H, W, C)
                for b in range(3)
            ]
            total = h_down(x[0]) + x[1] + h_up(x[2])
            top = row + (2 - a) * PLANE
            acc[top : top + rows, :] += total.reshape(rows, C)
        if turned is not None:
            for at in range(row, row + rows, C):
                for c in range(3):
                    block = source[at : at + C, c * C : (c + 1) * C]
                    turned[c * C : (c + 1) * C, at : at + C] = block.T


def by_taps(flat, weight):
    for k in range(TAPS):
        c, ab = k % 3, k // 3
        weight[c * C : (c + 1) * C, ab * C : (ab + 1) * C] = flat[
            k * C : (k + 1) * C, :
        ].astype(bf16)


def reverse_into(weight, out):
    for k in range(TAPS):
        c, ab = k % 3, k // 3
        block = weight[(2 - c) * C : (3 - c) * C, (8 - ab) * C : (9 - ab) * C]
        out[c * C : (c + 1) * C, ab * C : (ab + 1) * C] = block.T


def assemble(core, mine, theirs, flat, weight):
    chips = mine.shape[0]
    part = ROWS // (2 * chips)
    mine_first = core == 0
    for y in range(chips):
        one = mine[y].astype(f32)
        two = theirs[y].astype(f32)
        even = jnp.where(mine_first, one, two)[:part]
        odd = jnp.where(mine_first, two, one)[:part]
        flat[2 * y * part : (2 * y + 1) * part, :] = even
        flat[(2 * y + 1) * part : (2 * y + 2) * part, :] = odd
    by_taps(flat, weight)


def row_sum(x):
    return jnp.sum(x, axis=0, keepdims=True)


def grad_into(turned, delta, cells, flat, out, place, top):
    def shifted(a, first, last):
        row = (2 - a) * PLANE
        return delta[row : row + cells, first * C : last * C]

    jobs = [([(a, 0), (a, 1)], lambda a=a: shifted(a, 0, 2)) for a in range(3)]
    jobs.append(
        ([(0, 2), (1, 2)], lambda: jnp.concatenate([shifted(0, 2, 3), shifted(1, 2, 3)], axis=1))
    )
    jobs.append(([(2, 2)], lambda: shifted(2, 2, 3)))
    for taps, side in jobs:
        total = jnp.dot(turned[...], side(), preferred_element_type=f32)
        for n, (a, b) in enumerate(taps):
            for c in range(3):
                row = (9 * a + 3 * b + c) * C
                flat[row : row + C, :] = total[c * C : (c + 1) * C, n * C : (n + 1) * C]
    near, far, tall, _ = out.shape
    part = ROWS // (near * far)
    tall = tall // 2
    base = place[0] * (-(-part // SPLIT))
    for j in range(near * far):
        chunk = flat[pl.ds(j * part + base, tall), :].astype(bf16)
        out[j % near, j // near, top : top + tall, :] = chunk


def blocks_of(cells, body, init, rows=BLOCK):
    def one(i, carry):
        return body(i, pl.multiple_of(i * rows, rows), carry)

    return lax.fori_loop(0, cells // rows, one, init)


def statistics(conv, cells):
    zero = jnp.zeros((1, C), f32)

    def one(i, row, sums):
        acc = conv[pl.ds(row + PLANE, 4 * BLOCK), :]
        return (sums[0] + row_sum(acc), sums[1] + row_sum(acc * acc))

    total, square = blocks_of(cells, one, (zero, zero), 4 * BLOCK)
    average = total / cells
    return average, lax.rsqrt(square / cells - average * average + EPSILON)


def main_kernel(offsets, place, *refs):
    blocks, refs = refs[: len(offsets)], refs[len(offsets) :]
    (
        mine, theirs,
        output, outer_out, delta_out, grads_out, weight_out,
        image, cotangent, first_delta, outer_slab, grads,
        mine1, theirs1, mine2, theirs2, weight1, weight2, turned_weight,
        image_three, three, delta_three, image_turned, turned, normed, conv, conv2, outer, flat,
        image_sem, other_sem, weight_sem, out_sem,
    ) = refs
    cells = image.shape[0]
    planes = cells // PLANE
    slab = output.shape[0]
    count = cells // slab
    padded = mine1.shape[1]
    zero = jnp.zeros((1, C), f32)
    copy = pltpu.make_async_copy
    fields = ([], [])
    for n, ((offset, index), block) in enumerate(zip(offsets, blocks)):
        owner = lax.rem(place[0] + (offset + count), count)
        at = pl.ds(pl.multiple_of(owner * slab, slab), slab)
        row = 2 * index * slab
        fields[0].append(copy(block.at[row : row + slab], image.at[at], image_sem.at[n]))
        fields[1].append(
            copy(block.at[row + slab : row + 2 * slab], cotangent.at[at], other_sem.at[n])
        )
    weights = [
        copy(source.at[:, half * padded : (half + 1) * padded], target, weight_sem.at[n])
        for n, (source, half, target) in enumerate(
            ((mine, 0, mine1), (theirs, 0, theirs1), (mine, 1, mine2), (theirs, 1, theirs2))
        )
    ]
    for c in fields[0] + weights + fields[1]:
        c.start()
    edge = jnp.zeros((PLANE, 3 * C), bf16)
    delta_three[0:PLANE, :] = edge
    delta_three[cells + PLANE : cells + 2 * PLANE, :] = edge
    for c in fields[0]:
        c.wait()

    def each(row, body):
        for n in range(row, row + STEP * PLANE, BLOCK):
            body(n)

    def shift_image(n):
        put_w_shifts(image[n : n + BLOCK, :].astype(f32), image_three, n)

    for c in weights:
        c.wait()
    assemble(place[1], mine1, theirs1, flat, weight1)
    weight_copy = copy(weight1, weight_out, out_sem.at[0])
    weight_copy.start()
    conv_into(
        conv, image_three, weight1, planes, STEP, image_turned,
        lambda row: each(row, shift_image),
        lambda: assemble(place[1], mine2, theirs2, flat, weight2),
    )
    average1, inverse1 = statistics(conv, cells)

    def norm_one(n):
        u = (conv[n + PLANE : n + PLANE + BLOCK, :] - average1) * inverse1
        normed[n : n + BLOCK, :] = u
        put_w_shifts(u * phi_parts(u), three, n)

    conv_into(
        conv2, three, weight2, planes, STEP, turned,
        lambda row: each(row, norm_one),
        lambda: reverse_into(weight2, turned_weight),
    )
    average, inverse = statistics(conv2, cells)
    for c in fields[1]:
        c.wait()
    parts = slab // BLOCK

    def norm_two(i, row, sums):
        at = pl.ds(row, BLOCK)
        n = (conv2[pl.ds(row + PLANE, BLOCK), :] - average) * inverse
        conv2[pl.ds(row + PLANE, BLOCK), :] = n
        u = image[at, :].astype(f32) + n
        cdf = phi_parts(u)
        grad = cotangent[at, :].astype(f32) * slope_of(u, cdf)
        outer[at, :] = grad

        @pl.when(lax.div(i, parts) == place[0])
        def _():
            inner = pl.ds(pl.multiple_of(lax.rem(i, parts) * BLOCK, BLOCK), BLOCK)
            output[inner, :] = (u * cdf).astype(bf16)
            outer_slab[inner, :] = grad

        return (sums[0] + row_sum(grad), sums[1] + row_sum(grad * n))

    plain, paired = blocks_of(cells, norm_two, (zero, zero))
    outer_copy = copy(outer_slab, outer_out, out_sem.at[1])
    outer_copy.start()
    plain = plain / cells
    paired = paired / cells

    def back_two(i, row, _):
        n = conv2[pl.ds(row + PLANE, BLOCK), :]
        value = inverse * (outer[pl.ds(row, BLOCK), :] - plain - n * paired)
        put_w_shifts(value, three, row)
        put_h_shifts(value, delta_three, row + PLANE)
        return 0

    blocks_of(cells, back_two, 0)
    half = grads.shape[2] // 2
    grad_into(turned, delta_three, cells, flat, grads, place, half)

    conv_into(conv, three, turned_weight, planes, STEP)

    def inner_grad(i, row, sums):
        u = normed[pl.ds(row, BLOCK), :]
        grad = conv[pl.ds(row + PLANE, BLOCK), :] * slope_of(u, phi_parts(u))
        conv[pl.ds(row + PLANE, BLOCK), :] = grad
        return (sums[0] + row_sum(grad), sums[1] + row_sum(grad * u))

    plain1, paired1 = blocks_of(cells, inner_grad, (zero, zero))
    plain1 = plain1 / cells
    paired1 = paired1 / cells

    def back_one(i, row, _):
        at = pl.ds(row, BLOCK)
        grad = conv[pl.ds(row + PLANE, BLOCK), :]
        value = inverse1 * (grad - plain1 - normed[at, :] * paired1)
        first_delta[at, :] = value.astype(bf16)
        put_h_shifts(value, delta_three, row + PLANE)
        return 0

    blocks_of(cells, back_one, 0)
    delta_copy = copy(first_delta, delta_out, out_sem.at[2])
    delta_copy.start()
    grad_into(image_turned, delta_three, cells, flat, grads, place, 0)
    grads_copy = copy(grads, grads_out, out_sem.at[3])
    grads_copy.start()
    for c in (weight_copy, outer_copy, delta_copy, grads_copy):
        c.wait()


def fourth_kernel(place, delta, weight, outer_slab, grad, three, conv, turned_weight):
    slab = grad.shape[0]
    planes = slab // PLANE
    last = delta.shape[0] // PLANE
    reverse_into(weight, turned_weight)
    base = place[0] * planes
    for p in range(planes + 2):
        d = base + (p - 1)
        inside = jnp.logical_and(d >= 0, d < last)
        at = pl.multiple_of(jnp.clip(d, 0, last - 1) * PLANE, PLANE)
        x = delta[pl.ds(at, PLANE), :].astype(f32)
        put_w_shifts(jnp.where(inside, x, 0.0), three, p * PLANE)
    conv_into(conv, three, turned_weight, planes + 2, planes + 2)
    total = conv[2 * PLANE : 2 * PLANE + slab, :]
    grad[...] = (outer_slab[...] + total).astype(bf16)


SMEM = pl.BlockSpec(memory_space=pltpu.SMEM)
VMEM = pl.BlockSpec(memory_space=pltpu.VMEM)
HBM = pl.BlockSpec(memory_space=pltpu.HBM)


def call(kernel, outs, scratch, *args, mib=4, far_in=(), far_out=()):
    specs = [
        HBM if n in far_in else SMEM if a.dtype == jnp.int32 else VMEM
        for n, a in enumerate(args)
    ]
    args = [
        pltpu.with_memory_space_constraint(a, pltpu.HBM) if n in far_in else a
        for n, a in enumerate(args)
    ]
    return pl.pallas_call(
        kernel,
        out_shape=tuple(jax.ShapeDtypeStruct(s, d) for s, d in outs),
        in_specs=specs,
        out_specs=tuple(HBM if n in far_out else VMEM for n in range(len(outs))),
        scratch_shapes=scratch,
        compiler_params=pltpu.CompilerParams(vmem_limit_bytes=mib * 1024 * 1024),
    )(*args)


def main_call(place, blocks, mine, theirs, slab, chunks):
    count = sum(len(offsets) for offsets, _ in blocks)
    cells = slab * count
    offsets = [(o, n) for many, _ in blocks for n, o in enumerate(many)]
    arrays = [array for many, array in blocks for _ in many]
    field = (cells, C)
    half = (mine.shape[0], mine.shape[1] // 2, C)
    local = pltpu.VMEM
    signal = pltpu.SemaphoreType.DMA
    return call(
        functools.partial(main_kernel, offsets),
        [
            ((slab, C), bf16), ((slab, C), f32), (field, bf16), (chunks, bf16),
            ((3 * C, NINE), bf16),
        ],
        [local(field, bf16)] * 3
        + [local((slab, C), f32), local(chunks, bf16)]
        + [local(half, bf16)] * 4
        + [local((3 * C, NINE), bf16)] * 3
        + [
            local((cells, 3 * C), bf16), local((cells, 3 * C), bf16),
            local((cells + 2 * PLANE, 3 * C), bf16),
            local((3 * C, cells), bf16), local((3 * C, cells), bf16),
            local(field, f32), local((cells + 2 * PLANE, C), f32),
            local((cells + 2 * PLANE, C), f32), local(field, f32),
            local((ROWS + 8, C), f32),
            signal((count,)), signal((count,)), signal((4,)), signal((4,)),
        ],
        place, *arrays, mine, theirs,
        mib=32, far_in=range(1, count + 3), far_out=(1, 2, 3, 4),
    )


def fourth_call(place, delta, weight, outer_slab):
    slab = outer_slab.shape[0]
    return call(
        fourth_kernel,
        [((slab, C), bf16)],
        [
            pltpu.VMEM((slab + 2 * PLANE, 3 * C), bf16),
            pltpu.VMEM((slab + 4 * PLANE, C), f32),
            pltpu.VMEM((3 * C, NINE), bf16),
        ],
        place, delta, weight, outer_slab, mib=8,
    )[0]


def near_kernel(parts, out):
    total = jnp.sum(parts[...].astype(f32), axis=0).astype(bf16)
    far = parts.shape[1]
    copies = out.shape[0] // far
    for y in range(far):
        for n in range(copies):
            out[y * copies + n] = total[y]


def near_call(parts, copies):
    shape = (parts.shape[1] * copies,) + parts.shape[2:]
    return call(near_kernel, [(shape, bf16)], [], parts)[0]


def copies_kernel(first, second, out):
    part, padded = first.shape[0], out.shape[1] // 2
    gap = jnp.zeros((padded - part, C), bf16)
    rows = jnp.concatenate([first[...], gap, second[...], gap])
    for n in range(out.shape[0]):
        out[n] = rows


def copies_call(first, second, count, padded):
    return call(copies_kernel, [((count, 2 * padded, C), bf16)], [], first, second)[0]


def far_kernel(factor, parts, first, second):
    _, split, both, _ = parts.shape
    tall = both // 2
    part = first.shape[0]
    piece = -(-part // split)
    for s in range(split):
        total = jnp.sum(parts[:, s].astype(f32), axis=0) * factor
        rows = min(piece, part - s * piece)
        first[s * piece : s * piece + rows, :] = total[:rows]
        second[s * piece : s * piece + rows, :] = total[tall : tall + rows]


def far_call(parts, part, factor):
    return call(
        functools.partial(far_kernel, factor),
        [((part, C), f32), ((part, C), f32)], [], parts,
    )


def solution(mesh):
    dp, space = mesh.shape["dp"], mesh.shape["space"]
    across = 4
    fine = Mesh(
        mesh.devices.reshape(dp // (4 * across), 2, across, 2, space),
        ("pair", "y", "x", "core", "space"),
    )
    swap = [(0, 1), (1, 0)]
    near = 4 * across
    far = dp // near

    def shifted(x, hops):
        pairs = [((i + hops) % space, i) for i in range(space)]
        return lax.ppermute(x, "space", pairs)

    def whole_patch(x):
        blocks = [((0,), x)]
        up = down = x
        for hops in range(1, space // 2):
            up = shifted(up, 1)
            down = shifted(down, -1)
            blocks += [((hops,), up), ((-hops,), down)]
        return blocks + [((space // 2,), shifted(x, space // 2))]

    def step(image, cotangent, first_weight, second_weight):
        slab = image.shape[1] * PLANE
        cells = slab * space
        part = first_weight.shape[0]
        padded = -(-part // 8) * 8
        piece = -(-part // space)
        chunks = (near, far, 2 * (-(-piece // 8) * 8), C)
        factor = 1.0 / math.sqrt(cells * dp)
        core = lax.axis_index("core")
        place = jnp.stack([lax.axis_index("space"), core]).astype(jnp.int32)

        mine = lax.all_to_all(
            copies_call(first_weight, second_weight, dp // 2, padded),
            ("pair", "y", "x"), 0, 0, tiled=True,
        )
        pair = jnp.concatenate([image.reshape(slab, C), cotangent.reshape(slab, C)])
        blocks = whole_patch(pair)
        theirs = lax.ppermute(mine, "core", swap)
        output, outer_slab, first_delta, grads, w1 = main_call(
            place, blocks, mine, theirs, slab, chunks
        )
        parts = lax.all_to_all(grads, ("y", "x", "core"), 0, 0, tiled=True)
        image_grad = fourth_call(place, first_delta, w1, outer_slab)
        sums = near_call(parts, space)
        ends = lax.all_to_all(sums, ("pair", "space"), 0, 0, tiled=True)
        first_grad, second_grad = far_call(
            ends.reshape((far, space) + sums.shape[1:]), part, factor
        )
        return (
            output.reshape(image.shape),
            image_grad.reshape(image.shape),
            first_grad,
            second_grad,
        )

    dp_axes = ("pair", "y", "x", "core")
    field = P(dp_axes, "space", None, None, None)
    rows = P(dp_axes, None)
    return jax.shard_map(
        step,
        mesh=fine,
        in_specs=(field, field, rows, rows),
        out_specs=(field, field, rows, rows),
        check_vma=False,
    )
```

```python
import functools
import math

import jax
import jax.numpy as jnp
from jax import lax
from jax.experimental import pallas as pl
from jax.experimental.pallas import tpu as pltpu
from jax.sharding import Mesh, PartitionSpec as P


EPSILON = 1e-05
C = 128
H = 8
W = 8
PLANE = H * W
TAPS = 27
NINE = 9 * C
ROWS = TAPS * C
BLOCK = 128
STEP = 16
SPLIT = 8

bf16 = jnp.bfloat16
f32 = jnp.float32


def phi_parts(u):
    cdf = 0.5 * (1.0 + lax.erf(u * 0.7071067811865476))
    return cdf


def slope_of(u, cdf):
    return cdf + u * jnp.exp(-0.5 * u * u) * 0.3989422804014327


def put_w_shifts(value, out, row):
    rows = value.shape[0]
    x = value.reshape(rows // PLANE, H, W, C)
    w_at = lax.broadcasted_iota(jnp.int32, x.shape, 2)
    left = jnp.where(w_at >= 1, pltpu.roll(x, 1, axis=2), 0.0)
    right = jnp.where(w_at <= W - 2, pltpu.roll(x, W - 1, axis=2), 0.0)
    for c, y in enumerate((left, x, right)):
        out[pl.ds(row, rows), c * C : (c + 1) * C] = y.reshape(rows, C).astype(bf16)


def h_down(x):
    return jnp.concatenate([jnp.zeros_like(x[:, :1]), x[:, : H - 1]], axis=1)


def h_up(x):
    return jnp.concatenate([x[:, 1:], jnp.zeros_like(x[:, :1])], axis=1)


def put_h_shifts(value, out, row):
    rows = value.shape[0]
    x = value.reshape(rows // PLANE, H, W, C)
    for b, y in enumerate((h_up(x), x, h_down(x))):
        out[pl.ds(row, rows), b * C : (b + 1) * C] = y.reshape(rows, C).astype(bf16)


def conv_into(acc, source, weight, planes, step, turned=None):
    rows = step * PLANE

    margin = 2 * PLANE

    def clear(i, _):
        at = pl.ds(pl.multiple_of(i * margin, margin), margin)
        acc[at, :] = jnp.zeros((margin, C), f32)
        return 0

    lax.fori_loop(0, (planes + 2) // 2, clear, 0)

    def one(i, _):
        row = pl.multiple_of(i * rows, rows)
        z = jnp.dot(source[pl.ds(row, rows), :], weight[...], preferred_element_type=f32)
        for a in range(3):
            x = [
                z[:, (3 * a + b) * C : (3 * a + b + 1) * C].reshape(step, H, W, C)
                for b in range(3)
            ]
            total = h_down(x[0]) + x[1] + h_up(x[2])
            at = pl.ds(pl.multiple_of(row + (2 - a) * PLANE, PLANE), rows)
            acc[at, :] += total.reshape(rows, C)
        if turned is not None:
            for n in range(rows // C):
                at = pl.multiple_of(row + n * C, C)
                for c in range(3):
                    block = source[pl.ds(at, C), c * C : (c + 1) * C]
                    turned[c * C : (c + 1) * C, pl.ds(at, C)] = block.T
        return 0

    lax.fori_loop(0, planes // step, one, 0)


def by_taps(flat, weight):
    for k in range(TAPS):
        c, ab = k % 3, k // 3
        weight[c * C : (c + 1) * C, ab * C : (ab + 1) * C] = flat[
            k * C : (k + 1) * C, :
        ].astype(bf16)


def reverse_into(weight, out):
    for k in range(TAPS):
        c, ab = k % 3, k // 3
        block = weight[(2 - c) * C : (3 - c) * C, (8 - ab) * C : (9 - ab) * C]
        out[c * C : (c + 1) * C, ab * C : (ab + 1) * C] = block.T


def assemble(core, mine, theirs, flat, weight):
    chips = mine.shape[0]
    part = ROWS // (2 * chips)
    mine_first = core == 0
    for y in range(chips):
        one = mine[y].astype(f32)
        two = theirs[y].astype(f32)
        even = jnp.where(mine_first, one, two)[:part]
        odd = jnp.where(mine_first, two, one)[:part]
        flat[2 * y * part : (2 * y + 1) * part, :] = even
        flat[(2 * y + 1) * part : (2 * y + 2) * part, :] = odd
    by_taps(flat, weight)


def row_sum(x):
    return jnp.sum(x, axis=0, keepdims=True)


def grad_into(turned, delta, cells, flat, out, place, top):
    def shifted(a, first, last):
        row = (2 - a) * PLANE
        return delta[row : row + cells, first * C : last * C]

    jobs = [([(a, 0), (a, 1)], lambda a=a: shifted(a, 0, 2)) for a in range(3)]
    jobs.append(
        ([(0, 2), (1, 2)], lambda: jnp.concatenate([shifted(0, 2, 3), shifted(1, 2, 3)], axis=1))
    )
    jobs.append(([(2, 2)], lambda: shifted(2, 2, 3)))
    for taps, side in jobs:
        total = jnp.dot(turned[...], side(), preferred_element_type=f32)
        for n, (a, b) in enumerate(taps):
            for c in range(3):
                row = (9 * a + 3 * b + c) * C
                flat[row : row + C, :] = total[c * C : (c + 1) * C, n * C : (n + 1) * C]
    near, far, tall, _ = out.shape
    part = ROWS // (near * far)
    tall = tall // 2
    base = place[0] * (-(-part // SPLIT))
    for j in range(near * far):
        chunk = flat[pl.ds(j * part + base, tall), :].astype(bf16)
        out[j % near, j // near, top : top + tall, :] = chunk


def blocks_of(cells, body, init, rows=BLOCK):
    def one(i, carry):
        return body(i, pl.multiple_of(i * rows, rows), carry)

    return lax.fori_loop(0, cells // rows, one, init)


def statistics(conv, cells):
    zero = jnp.zeros((1, C), f32)

    def one(i, row, sums):
        acc = conv[pl.ds(row + PLANE, 4 * BLOCK), :]
        return (sums[0] + row_sum(acc), sums[1] + row_sum(acc * acc))

    total, square = blocks_of(cells, one, (zero, zero), 4 * BLOCK)
    average = total / cells
    return average, lax.rsqrt(square / cells - average * average + EPSILON)


def main_kernel(offsets, place, *refs):
    blocks, refs = refs[: len(offsets)], refs[len(offsets) :]
    (
        mine, theirs,
        output, outer_out, delta_out, grads_out, weight_out,
        image, cotangent, first_delta, outer_slab, grads,
        mine1, theirs1, mine2, theirs2, weight1, weight2, turned_weight,
        image_three, three, delta_three, image_turned, turned, normed, conv, outer, flat,
        image_sem, other_sem, weight_sem, out_sem,
    ) = refs
    cells = image.shape[0]
    planes = cells // PLANE
    slab = output.shape[0]
    count = cells // slab
    padded = mine1.shape[1]
    zero = jnp.zeros((1, C), f32)
    copy = pltpu.make_async_copy
    fields = ([], [])
    for n, ((offset, index), block) in enumerate(zip(offsets, blocks)):
        owner = lax.rem(place[0] + (offset + count), count)
        at = pl.ds(pl.multiple_of(owner * slab, slab), slab)
        row = 2 * index * slab
        fields[0].append(copy(block.at[row : row + slab], image.at[at], image_sem.at[n]))
        fields[1].append(
            copy(block.at[row + slab : row + 2 * slab], cotangent.at[at], other_sem.at[n])
        )
    weights = [
        copy(source.at[:, half * padded : (half + 1) * padded], target, weight_sem.at[n])
        for n, (source, half, target) in enumerate(
            ((mine, 0, mine1), (theirs, 0, theirs1), (mine, 1, mine2), (theirs, 1, theirs2))
        )
    ]
    for c in fields[0] + weights + fields[1]:
        c.start()
    edge = jnp.zeros((PLANE, 3 * C), bf16)
    delta_three[0:PLANE, :] = edge
    delta_three[cells + PLANE : cells + 2 * PLANE, :] = edge
    for c in fields[0]:
        c.wait()

    def shift_image(i, row, _):
        put_w_shifts(image[pl.ds(row, BLOCK), :].astype(f32), image_three, row)
        return 0

    blocks_of(cells, shift_image, 0)
    for c in weights[:2]:
        c.wait()
    assemble(place[1], mine1, theirs1, flat, weight1)
    weight_copy = copy(weight1, weight_out, out_sem.at[0])
    weight_copy.start()
    conv_into(conv, image_three, weight1, planes, STEP, image_turned)
    average1, inverse1 = statistics(conv, cells)

    def norm_one(i, row, _):
        u = (conv[pl.ds(row + PLANE, BLOCK), :] - average1) * inverse1
        normed[pl.ds(row, BLOCK), :] = u
        put_w_shifts(u * phi_parts(u), three, row)
        return 0

    blocks_of(cells, norm_one, 0)
    for c in weights[2:]:
        c.wait()
    assemble(place[1], mine2, theirs2, flat, weight2)
    conv_into(conv, three, weight2, planes, STEP, turned)
    average, inverse = statistics(conv, cells)
    for c in fields[1]:
        c.wait()
    parts = slab // BLOCK

    def norm_two(i, row, sums):
        at = pl.ds(row, BLOCK)
        n = (conv[pl.ds(row + PLANE, BLOCK), :] - average) * inverse
        conv[pl.ds(row + PLANE, BLOCK), :] = n
        u = image[at, :].astype(f32) + n
        cdf = phi_parts(u)
        grad = cotangent[at, :].astype(f32) * slope_of(u, cdf)
        outer[at, :] = grad

        @pl.when(lax.div(i, parts) == place[0])
        def _():
            inner = pl.ds(pl.multiple_of(lax.rem(i, parts) * BLOCK, BLOCK), BLOCK)
            output[inner, :] = (u * cdf).astype(bf16)
            outer_slab[inner, :] = grad

        return (sums[0] + row_sum(grad), sums[1] + row_sum(grad * n))

    plain, paired = blocks_of(cells, norm_two, (zero, zero))
    outer_copy = copy(outer_slab, outer_out, out_sem.at[1])
    outer_copy.start()
    plain = plain / cells
    paired = paired / cells

    def back_two(i, row, _):
        n = conv[pl.ds(row + PLANE, BLOCK), :]
        value = inverse * (outer[pl.ds(row, BLOCK), :] - plain - n * paired)
        put_w_shifts(value, three, row)
        put_h_shifts(value, delta_three, row + PLANE)
        return 0

    blocks_of(cells, back_two, 0)
    half = grads.shape[2] // 2
    grad_into(turned, delta_three, cells, flat, grads, place, half)

    reverse_into(weight2, turned_weight)
    conv_into(conv, three, turned_weight, planes, STEP)

    def inner_grad(i, row, sums):
        u = normed[pl.ds(row, BLOCK), :]
        grad = conv[pl.ds(row + PLANE, BLOCK), :] * slope_of(u, phi_parts(u))
        conv[pl.ds(row + PLANE, BLOCK), :] = grad
        return (sums[0] + row_sum(grad), sums[1] + row_sum(grad * u))

    plain1, paired1 = blocks_of(cells, inner_grad, (zero, zero))
    plain1 = plain1 / cells
    paired1 = paired1 / cells

    def back_one(i, row, _):
        at = pl.ds(row, BLOCK)
        grad = conv[pl.ds(row + PLANE, BLOCK), :]
        value = inverse1 * (grad - plain1 - normed[at, :] * paired1)
        first_delta[at, :] = value.astype(bf16)
        put_h_shifts(value, delta_three, row + PLANE)
        return 0

    blocks_of(cells, back_one, 0)
    delta_copy = copy(first_delta, delta_out, out_sem.at[2])
    delta_copy.start()
    grad_into(image_turned, delta_three, cells, flat, grads, place, 0)
    grads_copy = copy(grads, grads_out, out_sem.at[3])
    grads_copy.start()
    for c in (weight_copy, outer_copy, delta_copy, grads_copy):
        c.wait()


def fourth_kernel(place, delta, weight, outer_slab, grad, three, conv, turned_weight):
    slab = grad.shape[0]
    planes = slab // PLANE
    last = delta.shape[0] // PLANE
    reverse_into(weight, turned_weight)
    base = place[0] * planes
    for p in range(planes + 2):
        d = base + (p - 1)
        inside = jnp.logical_and(d >= 0, d < last)
        at = pl.multiple_of(jnp.clip(d, 0, last - 1) * PLANE, PLANE)
        x = delta[pl.ds(at, PLANE), :].astype(f32)
        put_w_shifts(jnp.where(inside, x, 0.0), three, p * PLANE)
    conv_into(conv, three, turned_weight, planes + 2, planes + 2)
    total = conv[2 * PLANE : 2 * PLANE + slab, :]
    grad[...] = (outer_slab[...] + total).astype(bf16)


SMEM = pl.BlockSpec(memory_space=pltpu.SMEM)
VMEM = pl.BlockSpec(memory_space=pltpu.VMEM)
HBM = pl.BlockSpec(memory_space=pltpu.HBM)


def call(kernel, outs, scratch, *args, mib=4, far_in=(), far_out=()):
    specs = [
        HBM if n in far_in else SMEM if a.dtype == jnp.int32 else VMEM
        for n, a in enumerate(args)
    ]
    args = [
        pltpu.with_memory_space_constraint(a, pltpu.HBM) if n in far_in else a
        for n, a in enumerate(args)
    ]
    return pl.pallas_call(
        kernel,
        out_shape=tuple(jax.ShapeDtypeStruct(s, d) for s, d in outs),
        in_specs=specs,
        out_specs=tuple(HBM if n in far_out else VMEM for n in range(len(outs))),
        scratch_shapes=scratch,
        compiler_params=pltpu.CompilerParams(vmem_limit_bytes=mib * 1024 * 1024),
    )(*args)


def main_call(place, blocks, mine, theirs, slab, chunks):
    count = sum(len(offsets) for offsets, _ in blocks)
    cells = slab * count
    offsets = [(o, n) for many, _ in blocks for n, o in enumerate(many)]
    arrays = [array for many, array in blocks for _ in many]
    field = (cells, C)
    half = (mine.shape[0], mine.shape[1] // 2, C)
    local = pltpu.VMEM
    signal = pltpu.SemaphoreType.DMA
    return call(
        functools.partial(main_kernel, offsets),
        [
            ((slab, C), bf16), ((slab, C), f32), (field, bf16), (chunks, bf16),
            ((3 * C, NINE), bf16),
        ],
        [local(field, bf16)] * 3
        + [local((slab, C), f32), local(chunks, bf16)]
        + [local(half, bf16)] * 4
        + [local((3 * C, NINE), bf16)] * 3
        + [
            local((cells, 3 * C), bf16), local((cells, 3 * C), bf16),
            local((cells + 2 * PLANE, 3 * C), bf16),
            local((3 * C, cells), bf16), local((3 * C, cells), bf16),
            local(field, f32), local((cells + 2 * PLANE, C), f32), local(field, f32),
            local((ROWS + 8, C), f32),
            signal((count,)), signal((count,)), signal((4,)), signal((4,)),
        ],
        place, *arrays, mine, theirs,
        mib=32, far_in=range(1, count + 3), far_out=(1, 2, 3, 4),
    )


def fourth_call(place, delta, weight, outer_slab):
    slab = outer_slab.shape[0]
    return call(
        fourth_kernel,
        [((slab, C), bf16)],
        [
            pltpu.VMEM((slab + 2 * PLANE, 3 * C), bf16),
            pltpu.VMEM((slab + 4 * PLANE, C), f32),
            pltpu.VMEM((3 * C, NINE), bf16),
        ],
        place, delta, weight, outer_slab, mib=8,
    )[0]


def near_kernel(parts, out):
    total = jnp.sum(parts[...].astype(f32), axis=0).astype(bf16)
    far = parts.shape[1]
    copies = out.shape[0] // far
    for y in range(far):
        for n in range(copies):
            out[y * copies + n] = total[y]


def near_call(parts, copies):
    shape = (parts.shape[1] * copies,) + parts.shape[2:]
    return call(near_kernel, [(shape, bf16)], [], parts)[0]


def copies_kernel(first, second, out):
    part, padded = first.shape[0], out.shape[1] // 2
    gap = jnp.zeros((padded - part, C), bf16)
    rows = jnp.concatenate([first[...], gap, second[...], gap])
    for n in range(out.shape[0]):
        out[n] = rows


def copies_call(first, second, count, padded):
    return call(copies_kernel, [((count, 2 * padded, C), bf16)], [], first, second)[0]


def far_kernel(factor, parts, first, second):
    _, split, both, _ = parts.shape
    tall = both // 2
    part = first.shape[0]
    piece = -(-part // split)
    for s in range(split):
        total = jnp.sum(parts[:, s].astype(f32), axis=0) * factor
        rows = min(piece, part - s * piece)
        first[s * piece : s * piece + rows, :] = total[:rows]
        second[s * piece : s * piece + rows, :] = total[tall : tall + rows]


def far_call(parts, part, factor):
    return call(
        functools.partial(far_kernel, factor),
        [((part, C), f32), ((part, C), f32)], [], parts,
    )


def solution(mesh):
    dp, space = mesh.shape["dp"], mesh.shape["space"]
    across = 4
    fine = Mesh(
        mesh.devices.reshape(dp // (4 * across), 2, across, 2, space),
        ("pair", "y", "x", "core", "space"),
    )
    swap = [(0, 1), (1, 0)]
    near = 4 * across
    far = dp // near

    def shifted(x, hops):
        pairs = [((i + hops) % space, i) for i in range(space)]
        return lax.ppermute(x, "space", pairs)

    def whole_patch(x):
        blocks = [((0,), x)]
        up = down = x
        for hops in range(1, space // 2):
            up = shifted(up, 1)
            down = shifted(down, -1)
            blocks += [((hops,), up), ((-hops,), down)]
        return blocks + [((space // 2,), shifted(x, space // 2))]

    def step(image, cotangent, first_weight, second_weight):
        slab = image.shape[1] * PLANE
        cells = slab * space
        part = first_weight.shape[0]
        padded = -(-part // 8) * 8
        piece = -(-part // space)
        chunks = (near, far, 2 * (-(-piece // 8) * 8), C)
        factor = 1.0 / math.sqrt(cells * dp)
        core = lax.axis_index("core")
        place = jnp.stack([lax.axis_index("space"), core]).astype(jnp.int32)

        mine = lax.all_to_all(
            copies_call(first_weight, second_weight, dp // 2, padded),
            ("pair", "y", "x"), 0, 0, tiled=True,
        )
        pair = jnp.concatenate([image.reshape(slab, C), cotangent.reshape(slab, C)])
        blocks = whole_patch(pair)
        theirs = lax.ppermute(mine, "core", swap)
        output, outer_slab, first_delta, grads, w1 = main_call(
            place, blocks, mine, theirs, slab, chunks
        )
        parts = lax.all_to_all(grads, ("y", "x", "core"), 0, 0, tiled=True)
        image_grad = fourth_call(place, first_delta, w1, outer_slab)
        sums = near_call(parts, space)
        ends = lax.all_to_all(sums, ("pair", "space"), 0, 0, tiled=True)
        first_grad, second_grad = far_call(
            ends.reshape((far, space) + sums.shape[1:]), part, factor
        )
        return (
            output.reshape(image.shape),
            image_grad.reshape(image.shape),
            first_grad,
            second_grad,
        )

    dp_axes = ("pair", "y", "x", "core")
    field = P(dp_axes, "space", None, None, None)
    rows = P(dp_axes, None)
    return jax.shard_map(
        step,
        mesh=fine,
        in_specs=(field, field, rows, rows),
        out_specs=(field, field, rows, rows),
        check_vma=False,
    )
```
